512 devices in a mesh: mer: 128 (over z, y, core), az: 4 (over x).
Axes of the slice: x: 4, y: 8, z: 8, core: 2. Of those that a mesh axis runs over, the one named last changes fastest.
Arguments:
- displacement: float32 [3, 5, 1024, 512], P(None, None, 'mer', 'az'), may hold values from -6 to 6
- velocity: float32 [3, 5, 1024, 512], P(None, None, 'mer', 'az'), may hold values from -1.5 to 1.5
- modulus: float32 [1, 256], P(None, 'mer'), may hold values from 0.5 to 2
- hoop_strength: float32 [1, 256], P(None, 'mer'), may hold values from 0.5 to 2
- coupling: float32 [1, 256], P(None, 'mer'), may hold values from -1 to 1
- density: float32 [1, 256], P(None, 'mer'), may hold values from 0.5 to 2
- order_count: int32 [1, 256], P(None, 'mer'), may hold values from 1 to 256
- point_element: int32 [8192, 2], P('mer'), may hold values from 0 to 255, as said below
- point_local: float32 [8192, 2], P('mer'), may hold values from -1 to 1
- azimuth_scale: float32 [8192], P('mer'), may hold values from 0.5 to 2
- point_owner: int32 [8192, 1], P('mer'), may hold values from 0 to 127; in each aligned block of 64 rows (0 to 63, 64 to 127, ...) at most 2 rows name the same one
- point_cell: int32 [8192], P('mer'), may hold values from 0 to 31
- adjoint_strain: float32 [9, 8, 512, 512], P(None, None, 'mer', 'az'), may hold values from -6 to 6
Outputs:
- final_displacement: float32 [3, 5, 1024, 512], P(None, None, 'mer', 'az')
- kernel: float32 [8, 512, 512], P(None, 'mer', 'az')
The draws below stay inside these ranges and needn't reach their ends.
Inputs may be any that keep to these rules, and one draw needn't show every extreme that they name: `point_element`: points p with p // 64 = i lie in colatitude elements i * 2 to (i + 1) * 2 - 1; the first column is below 1. `point_owner`: among the points of one device (aligned blocks of 64 points) no owner is named more than 2 times, a bound that some block reaches.
All inputs are finite; a program needn't handle non-finite values.
Results may differ from the reference program's by a relative error of at most 0.0003.
Values sent between devices are 32-bit elements; how exact they have to be, the bound alone decides.
No kernel may reach another device: no remote copies, remote signals or barrier semaphores. Data moves between devices by JAX's collectives and lax.ppermute only.
A program may use at most 64 MiB of HBM per device.

```python
import math
import jax
import jax.numpy as jnp
import numpy as np
from jax import lax

ER = 1
EC_DEV = 2
POINTS_DEV = 64
ORDERS = 256
STEPS = 3
VDEPTH = 8
VLAT_DEV = 4
EC = 256
NR = 5
NC = 1024
COEFS = 512
NPHI = 512
POINTS = 8192
CAP = 2
VLAT = 512
N_MER = 128
N_AZ = 4


def draw_point_element(key, part):
    key_rows, key_cols = jax.random.split(jax.random.fold_in(key, 17))
    row_draw = jax.random.randint(key_rows, (POINTS,), 0, ER, dtype=jnp.int32)
    device_of = jnp.arange(POINTS, dtype=jnp.int32) // POINTS_DEV
    col_draw = device_of * EC_DEV + jax.random.randint(key_cols, (POINTS,), 0, EC_DEV, dtype=jnp.int32)
    return jnp.stack([row_draw, col_draw], axis=1).astype(jnp.int32)


def plant(values, stream_key, least, high):
    longest = values.shape.index(max(values.shape))
    spots = []
    for shift in (0, 1):
        where = [jax.random.randint(jax.random.fold_in(stream_key, axis), (), 0, length) for axis, length in enumerate(values.shape)]
        where[longest] = (where[longest] + shift) % values.shape[longest]
        spots.append(tuple(where))
    return values.at[spots[0]].set(least).at[spots[1]].set(high)


def shard_levels(rng, dims, cuts, low, high):
    level, own = 1.0, jax.random.fold_in(rng, 6)
    for dim, shards_of in cuts:
        steps = jnp.exp(jax.random.uniform(jax.random.fold_in(own, dim), (shards_of,), jnp.float32, low / len(cuts), high / len(cuts)))
        level = level * jnp.repeat(steps, dims[dim] // shards_of).reshape([-1 if axis == dim else 1 for axis in range(len(dims))])
    return level


def assign_block(stream_key, own, number, rows, number_of, top, limit, skew):
    order = jax.random.permutation(stream_key, number_of)
    packed, usual = portions_of(number_of, rows * top, limit, skew, True), portions_of(number_of, rows * top, limit, skew, False)
    places = jnp.arange(number_of)

    def named(lengths, rotation):
        used = int((lengths > 0).sum())
        fixed = max(1, used // 4)
        shifted = fixed + (places - fixed + rotation * (used - fixed)) % max(1, number_of - fixed)
        return jnp.zeros((number_of,), jnp.int32).at[order[jnp.where(places < fixed, places, shifted)]].set(jnp.asarray(lengths, jnp.int32))

    lengths = jnp.where(number % 4 == 0, named(packed, number // 4), named(usual, number - number // 4 - 1))
    mixed = jax.random.permutation(jax.random.fold_in(own, 3), number_of)
    giver, taker = mixed[0:number_of // 2 * 2:2], mixed[1:number_of // 2 * 2:2]
    room = jnp.minimum(lengths[giver] - 1, limit - lengths[taker]) // 2
    room = jnp.where((giver == order[0]) | (taker == order[0]) | (lengths[taker] == 0), 0, jnp.maximum(room, 0))
    shifted = jax.random.randint(jax.random.fold_in(own, 4), (number_of // 2,), 0, 1 << 20) % (room + 1)
    lengths = lengths.at[giver].add(-shifted).at[taker].add(shifted)
    labels = jnp.searchsorted(jnp.cumsum(lengths), jnp.arange(rows * top), side="right").astype(jnp.int32)
    grid = labels.reshape(top, rows).T
    grid = grid[jax.random.permutation(jax.random.fold_in(own, 1), rows)]
    rotation = jax.random.randint(jax.random.fold_in(own, 2), (rows, 1), 0, top)
    return jnp.take_along_axis(grid, (jnp.arange(top)[None, :] + rotation) % top, axis=1)


def portions_of(amount, total, reach, slope, full):
    weights = [(1 << 20) // math.isqrt(rank ** slope) + 1 for rank in range(1, amount + 1)]
    largest = reach if full else min(reach, max(-(-total // amount), total * weights[0] // sum(weights)))
    least = 1 if total - largest >= amount - 1 else 0
    counts, rest = [largest] + [least] * (amount - 1), total - largest - least * (amount - 1)
    while rest > 0:
        movable = [i for i in range(1, amount) if counts[i] < largest] or [i for i in range(1, amount) if counts[i] < reach]
        mass, remaining = sum([weights[i] for i in movable]), rest
        for i in movable:
            extra = min(reach - counts[i], max(1, remaining * weights[i] // mass), rest)
            counts[i] = counts[i] + extra
            rest = rest - extra
    return np.array(counts)


def gaussian(key, dims, width, limit, cuts=(), kind=jnp.bfloat16):
    entries = width * jax.random.normal(key, dims, jnp.float32)
    if cuts:
        entries = entries * shard_levels(key, dims, cuts, -0.22, 0.18)
    return jnp.clip(entries, -limit, limit).astype(kind)


def setup_inputs(seed: int = 0) -> dict:
    key_list = jax.random.split(jax.random.key(seed), 14)
    displacement = gaussian(key_list[0], (3, NR, NC, COEFS), 1.0, 6.0, ((2, 128), (3, 4)), jnp.float32)
    velocity = gaussian(key_list[1], (3, NR, NC, COEFS), 0.25, 1.5, ((2, 128), (3, 4)), jnp.float32)
    modulus = jnp.clip(jnp.exp(math.log(2.0) - 1.3862944 * jax.random.uniform(key_list[2], (ER, EC), jnp.float32) ** shard_levels(key_list[2], (ER, EC), ((1, 128),), -0.2, 0.2)), 0.5, 2.0)
    hoop_strength = jnp.clip(jnp.exp(math.log(2.0) - 1.3862944 * jax.random.uniform(key_list[3], (ER, EC), jnp.float32) ** shard_levels(key_list[3], (ER, EC), ((1, 128),), -0.2, 0.2)), 0.5, 2.0)
    coupling = jnp.clip(jax.random.uniform(key_list[4], (ER, EC), jnp.float32, -1.0, 1.0) * shard_levels(key_list[4], (ER, EC), ((1, 128),), -0.4, 0.0), -1.0, 1.0)
    density = jnp.clip(jnp.exp(math.log(2.0) - 1.3862944 * jax.random.uniform(key_list[5], (ER, EC), jnp.float32) ** shard_levels(key_list[5], (ER, EC), ((1, 128),), -0.2, 0.2)), 0.5, 2.0)
    order_count = plant(jax.random.randint(key_list[6], (ER, EC), 1, ORDERS + 1), jax.random.fold_in(key_list[6], 1), 1, ORDERS).astype(jnp.int32)
    point_element = draw_point_element(jax.random.fold_in(key_list[13], 71), 0)
    point_local = jnp.clip(jax.random.uniform(key_list[8], (POINTS, 2), jnp.float32, -1.0, 1.0) * shard_levels(key_list[8], (POINTS, 2), ((0, 128),), -0.4, 0.0), -1.0, 1.0)
    azimuth_scale = jnp.clip(jnp.exp(math.log(2.0) - 1.3862944 * jax.random.uniform(key_list[9], (POINTS,), jnp.float32) ** shard_levels(key_list[9], (POINTS,), ((0, 128),), -0.2, 0.2)), 0.5, 2.0)
    point_owner_keys = jax.random.split(jax.random.fold_in(key_list[10], 1), POINTS // POINTS_DEV)
    point_owner_turns = jax.random.permutation(jax.random.fold_in(key_list[10], 3), POINTS // POINTS_DEV)
    point_owner = jax.vmap(lambda own, number: assign_block(jax.random.fold_in(key_list[10], 2), own, number, POINTS_DEV, N_MER, 1, CAP, 2))(point_owner_keys, point_owner_turns).reshape((POINTS, 1))
    point_cell = plant(jax.random.randint(key_list[11], (POINTS,), 0, VDEPTH * VLAT_DEV), jax.random.fold_in(key_list[11], 1), 0, (VDEPTH * VLAT_DEV) - 1).astype(jnp.int32)
    adjoint_strain = gaussian(key_list[12], (9, VDEPTH, VLAT, NPHI), 1.0, 6.0, ((2, 128), (3, 4)), jnp.float32)
    return dict(displacement=displacement, velocity=velocity, modulus=modulus, hoop_strength=hoop_strength, coupling=coupling, density=density, order_count=order_count, point_element=point_element, point_local=point_local, azimuth_scale=azimuth_scale, point_owner=point_owner, point_cell=point_cell, adjoint_strain=adjoint_strain)


step_scale = 0.015
smooth_rate = 0.125

def gll_tables():
    gll_nodes = np.array([-1.0, -math.sqrt(3.0 / 7.0), 0.0, math.sqrt(3.0 / 7.0), 1.0])
    gll_weights = np.array([0.1, 49.0 / 90.0, 32.0 / 45.0, 49.0 / 90.0, 0.1])
    derivative = np.zeros((5, 5))
    for i in range(5):
        for j in range(5):
            if i == j:
                derivative[i, j] = sum((1.0 / (gll_nodes[i] - gll_nodes[l]) for l in range(5) if l != i))
            else:
                scale_i = np.prod([gll_nodes[i] - gll_nodes[l] for l in range(5) if l != i])
                scale_j = np.prod([gll_nodes[j] - gll_nodes[l] for l in range(5) if l != j])
                derivative[i, j] = scale_i / (scale_j * (gll_nodes[i] - gll_nodes[j]))
    return (gll_nodes, gll_weights, derivative)

def lagrange(position):
    gll_nodes = gll_tables()[0]
    basis_values = []
    basis_slopes = []
    for j in range(5):
        others = [l for l in range(5) if l != j]
        product = jnp.ones_like(position)
        for l in others:
            product = product * (position - float(gll_nodes[l])) / float(gll_nodes[j] - gll_nodes[l])
        gradient_sum = jnp.zeros_like(position)
        for l in others:
            summand = jnp.ones_like(position) / float(gll_nodes[j] - gll_nodes[l])
            for i in others:
                if i != l:
                    summand = summand * (position - float(gll_nodes[i])) / float(gll_nodes[j] - gll_nodes[i])
            gradient_sum = gradient_sum + summand
        basis_values.append(product)
        basis_slopes.append(gradient_sum)
    return (jnp.stack(basis_values, axis=1), jnp.stack(basis_slopes, axis=1))

def to_elements(nodal):
    count_rows = (nodal.shape[1] - 1) // 4
    count_cols = (nodal.shape[2] - 1) // 4
    radial = jnp.stack([nodal[:, a:a + 4 * count_rows:4] for a in range(5)], axis=2)
    return jnp.stack([radial[:, :, :, b:b + 4 * count_cols:4] for b in range(5)], axis=4)

def from_elements(element_values):
    components, count_rows, _, count_cols, _, coef_width = element_values.shape
    radial = jnp.zeros((components, 4 * count_rows + 1, count_cols, 5, coef_width), element_values.dtype)
    for a in range(5):
        radial = radial.at[:, a:a + 4 * count_rows:4].add(element_values[:, :, a])
    assembled = jnp.zeros((components, 4 * count_rows + 1, 4 * count_cols + 1, coef_width), element_values.dtype)
    for b in range(5):
        assembled = assembled.at[:, :, b:b + 4 * count_cols:4].add(radial[:, :, :, b])
    return assembled

def quadrature_table():
    gll_weights = jnp.asarray(gll_tables()[1], jnp.float32)
    return gll_weights[:, None] * gll_weights[None, :]

def rotate(vector, order_ratio):
    lane_index = lax.broadcasted_iota(jnp.int32, vector.shape, vector.ndim - 1)
    is_even = lane_index % 2 == 0
    return jnp.where(is_even, jnp.roll(vector, -1, axis=-1), -jnp.roll(vector, 1, axis=-1)) * order_ratio

def element_mass(density):
    quadrature = quadrature_table()
    return (density[:, None, :, None] * quadrature[None, :, None, :])[None, :, :, :, :, None]

def element_forces(element_values, modulus, hoop_strength, coupling, order_count, order_index, order_ratio):
    quadrature = quadrature_table()
    derivative = jnp.asarray(gll_tables()[2], jnp.float32)
    highest = lax.Precision.HIGHEST

    def spread(per_element):
        return (per_element[:, None, :, None] * quadrature[None, :, None, :])[:, :, :, :, None]
    stiff_node = spread(modulus)[None]
    hoop_node = spread(hoop_strength)[None]
    couple_node = spread(coupling)
    grad_radial = jnp.einsum('pa,cEaFbk->cEpFbk', derivative, element_values, precision=highest)
    grad_colat = jnp.einsum('qb,cEaFbk->cEaFqk', derivative, element_values, precision=highest)
    back_radial = jnp.einsum('pa,cEpFbk->cEaFbk', derivative, stiff_node * grad_radial, precision=highest)
    back_colat = jnp.einsum('qb,cEaFqk->cEaFbk', derivative, stiff_node * grad_colat, precision=highest)
    forces = -(back_radial + back_colat + hoop_node * (order_ratio * order_ratio) * element_values)
    forces = jnp.stack([forces[0] + couple_node * rotate(element_values[2], order_ratio), forces[1], forces[2] - couple_node * rotate(element_values[0], order_ratio)], axis=0)
    order_mask = order_index[None, None, None, None, :] < order_count[:, None, :, None, None]
    return jnp.where(order_mask[None], forces, 0.0)

def point_gradients(gathered, xi_values, xi_slopes, eta_values, eta_slopes, azimuth_scale, order_ratio):
    highest = lax.Precision.HIGHEST
    nodal_value = jnp.einsum('pa,pb,cpabk->pck', xi_values, eta_values, gathered, precision=highest)
    along_radius = jnp.einsum('pa,pb,cpabk->pck', xi_slopes, eta_values, gathered, precision=highest)
    along_colat = jnp.einsum('pa,pb,cpabk->pck', xi_values, eta_slopes, gathered, precision=highest)
    around_axis = azimuth_scale[:, None, None] * rotate(nodal_value, order_ratio)
    stacked = jnp.stack([along_radius, along_colat, around_axis], axis=2)
    return stacked.reshape(gathered.shape[1], 9, gathered.shape[4])

def fourier_basis(coef_start, coef_count, phi_start, phi_count, total_phi):
    coef_rows = coef_start + lax.broadcasted_iota(jnp.int32, (coef_count, phi_count), 0)
    phi_cols = phi_start + lax.broadcasted_iota(jnp.int32, (coef_count, phi_count), 1)
    wrapped = coef_rows // 2 * phi_cols % total_phi
    angles = wrapped.astype(jnp.float32) * (2.0 * math.pi / total_phi)
    return jnp.where(coef_rows % 2 == 0, jnp.cos(angles), jnp.sin(angles))

def reference(displacement, velocity, modulus, hoop_strength, coupling, density, order_count, point_element, point_local, azimuth_scale, point_owner, point_cell, adjoint_strain):
    highest = lax.Precision.HIGHEST
    block_width = COEFS // N_AZ
    block_total = COEFS // block_width
    nodal_mass = from_elements(element_mass(density))[0, :, :NC]
    xi_values, xi_slopes = lagrange(point_local[:, 0])
    eta_values, eta_slopes = lagrange(point_local[:, 1])
    offsets = jnp.arange(5, dtype=jnp.int32)[None, :]
    row_index = 4 * point_element[:, 0:1] + offsets
    col_index = 4 * point_element[:, 1:2] + offsets

    def one_block(block_number):
        first_coef = block_number * block_width
        current = lax.dynamic_slice_in_dim(displacement, first_coef, block_width, 3)
        previous = current - lax.dynamic_slice_in_dim(velocity, first_coef, block_width, 3)
        order_index = (first_coef + jnp.arange(block_width, dtype=jnp.int32)) // 2
        order_ratio = order_index.astype(jnp.float32) / ORDERS
        closing = jnp.zeros((3, NR, 1, block_width), jnp.float32)
        for step_index in range(STEPS):
            padded = jnp.concatenate([current, closing], axis=2)
            forces = from_elements(element_forces(to_elements(padded), modulus, hoop_strength, coupling, order_count, order_index, order_ratio))[:, :, :NC]
            following = 2.0 * current - previous + step_scale * forces / nodal_mass
            previous, current = (current, following)
        padded = jnp.concatenate([current, closing], axis=2)
        gathered = padded[:, row_index[:, :, None], col_index[:, None, :], :]
        gradients = point_gradients(gathered, xi_values, xi_slopes, eta_values, eta_slopes, azimuth_scale, order_ratio)
        return (current, gradients)
    finals, gradients = lax.map(one_block, jnp.arange(block_total, dtype=jnp.int32))
    final_displacement = jnp.moveaxis(finals, 0, 3).reshape(3, NR, NC, COEFS)
    gradients = jnp.moveaxis(gradients, 0, 2).reshape(POINTS, 9, COEFS)
    basis = fourier_basis(0, COEFS, 0, NPHI, NPHI)
    samples = jnp.einsum('pgk,kj->pgj', gradients, basis, precision=highest) * (1.0 / math.sqrt(ORDERS))
    depth = point_cell // VLAT_DEV
    latitude = point_owner[:, 0] * VLAT_DEV + point_cell % VLAT_DEV
    adjoint_points = adjoint_strain[:, depth, latitude, :]
    contribution = lax.optimization_barrier(jnp.sum(samples * jnp.moveaxis(adjoint_points, 0, 1), axis=1))
    flat_voxel = depth * VLAT + latitude
    raw = jax.ops.segment_sum(contribution, flat_voxel, num_segments=VDEPTH * VLAT).reshape(VDEPTH, VLAT, NPHI)
    framed = jnp.pad(raw, ((1, 1), (1, 1), (0, 0)))
    neighbours = framed[2:, 1:-1] + framed[:-2, 1:-1] + framed[1:-1, 2:] + framed[1:-1, :-2]
    neighbours = neighbours + jnp.roll(raw, 1, axis=2) + jnp.roll(raw, -1, axis=2)
    kernel = raw + smooth_rate * (neighbours - 6.0 * raw)
    return (final_displacement, kernel)
```

```python
import math

import jax
import jax.numpy as jnp
import numpy as np
from jax import lax
from jax.experimental import pallas as pl
from jax.experimental.pallas import tpu as pltpu
from jax.sharding import Mesh
from jax.sharding import PartitionSpec as P

ORDERS = 256
STEPS = 3
MER = ("mer_0", "mer_1", "mer_2")
SIDES = ("mer_0", "mer_1")

step_scale = 0.015
smooth_rate = 0.125


def gll_tables():
    nodes = np.array([-1.0, -math.sqrt(3.0 / 7.0), 0.0, math.sqrt(3.0 / 7.0), 1.0])
    weights = np.array([0.1, 49.0 / 90.0, 32.0 / 45.0, 49.0 / 90.0, 0.1])
    derivative = np.zeros((5, 5))
    for i in range(5):
        for j in range(5):
            if i == j:
                derivative[i, j] = sum(1.0 / (nodes[i] - nodes[l]) for l in range(5) if l != i)
            else:
                scale_i = np.prod([nodes[i] - nodes[l] for l in range(5) if l != i])
                scale_j = np.prod([nodes[j] - nodes[l] for l in range(5) if l != j])
                derivative[i, j] = scale_i / (scale_j * (nodes[i] - nodes[j]))
    return nodes, weights, derivative


def stiffness_rows():
    _, weights, derivative = gll_tables()
    return (derivative.T @ np.diag(weights) @ derivative) / weights[:, None]


def basis_tables(blocks):
    k = np.arange(2 * ORDERS)
    order = k // 2
    width = 2 * ORDERS // blocks
    j = np.arange(2 * ORDERS)
    angle = (order[:, None] * j[None, :] % (2 * ORDERS)) * (2.0 * math.pi / (2 * ORDERS))
    even = (k % 2 == 0)[:, None]
    value = np.where(even, np.cos(angle), np.sin(angle)) / math.sqrt(ORDERS)
    slope = np.where(even, -np.sin(angle), np.cos(angle)) * (order[:, None] / ORDERS) / math.sqrt(ORDERS)
    table = np.stack([
        np.concatenate([value[:, b * width:(b + 1) * width], slope[:, b * width:(b + 1) * width]], axis=1)
        for b in range(blocks)
    ]).astype(np.float32)
    high = table.astype(jnp.bfloat16)
    low = (table - high.astype(np.float32)).astype(jnp.bfloat16)
    return np.stack([high, low], axis=1)


def lane_tables():
    nodes = gll_tables()[0]
    rows = np.zeros((16, 256), np.float32)
    for r in range(135):
        if r < 120:
            s, a, c = r // 40, r // 8 % 5, r % 8
        else:
            s, a, c = (r - 120) // 5, (r - 120) % 5, 8

        def place(first, n):
            others = [l for l in range(5) if l != n]
            for i, l in enumerate(others):
                rows[first + i, r] = nodes[l]
            rows[first + 4, r] = 1.0 / np.prod([nodes[n] - nodes[l] for l in others])

        place(0, a)
        if c <= 4:
            place(5, c)
        if c >= 4:
            place(10, c - 4)
        rows[15, r] = s + 1
    return rows


def split(x):
    high = x.astype(jnp.bfloat16)
    low = (x - high.astype(jnp.float32)).astype(jnp.bfloat16)
    return high, low


def dot(a, b):
    return jnp.dot(a, b, preferred_element_type=jnp.float32)


def pack_kernel(u_ref, v_ref, mod_ref, hoop_ref, coup_ref, dens_ref, count_ref, own_ref, up_ref, down_ref):
    own_ref[30:32] = jnp.zeros((2, 8, 128), jnp.float32)
    up_ref[7] = jnp.zeros((8, 128), jnp.float32)
    up_ref[8] = jnp.zeros((8, 128), jnp.float32)
    down_ref[15] = jnp.zeros((8, 128), jnp.float32)
    for i in range(15):
        u, v = u_ref[i], v_ref[i]
        own_ref[i] = u
        own_ref[15 + i] = v
        up_ref[i // 2, 4 * (i % 2):4 * (i % 2) + 4, :] = u_ref[i, 4:8, :]
        down_ref[i] = u
        down_ref[i, 5:6, :] = v_ref[i, 0:1, :]
    for i, ref in enumerate((mod_ref, hoop_ref, coup_ref, dens_ref, count_ref)):
        both = ref[...].astype(jnp.float32)
        first = jnp.broadcast_to(both[:, 0:1], (1, 128))
        second = jnp.broadcast_to(both[:, 1:2], (1, 128))
        own_ref[30, i:i + 1, :] = first
        own_ref[31, i:i + 1, :] = second
        down_ref[15, i:i + 1, :] = first
        up_ref[8, i:i + 1, :] = second


def pack(u, v, *coefs):
    f32 = jnp.float32
    return pl.pallas_call(
        pack_kernel,
        out_shape=(
            jax.ShapeDtypeStruct((32, 8, 128), f32),
            jax.ShapeDtypeStruct((9, 8, 128), f32),
            jax.ShapeDtypeStruct((16, 8, 128), f32),
        ),
        name="pack",
    )(u, v, *coefs)


def step_kernel(place_ref, own_ref, sib_ref, cross_ref, low_ref, high_ref, u_ref, gather_ref,
                ucol, vcol, coef, state, field):
    core, az = place_ref[0], place_ref[1]
    is_low = core == 0

    def left(i):
        return jnp.where(is_low, cross_ref[i], sib_ref[i])

    def right(i):
        return jnp.where(is_low, sib_ref[i], cross_ref[i])

    zero4 = jnp.zeros((4, 128), jnp.float32)
    zero8 = jnp.zeros((8, 128), jnp.float32)
    for i in range(15):
        ucol[i, 0:8, :] = zero8
        ucol[i, 4:8, :] = low_ref[i // 2, 4 * (i % 2):4 * (i % 2) + 4, :]
        ucol[i, 8:16, :] = left(i)
        ucol[i, 16:24, :] = own_ref[i]
        ucol[i, 24:32, :] = right(i)
        ucol[i, 32:40, :] = high_ref[i]
        vcol[i, 0:8, :] = zero8
        vcol[i, 8:16, :] = left(15 + i)
        vcol[i, 16:24, :] = own_ref[15 + i]
        vcol[i, 24:32, :] = right(15 + i)
        vcol[i, 32:40, :] = zero8
        vcol[i, 32:33, :] = high_ref[i, 5:6, :]
    l0, l1, r0, r1 = left(30), left(31), right(30), right(31)
    sources = (low_ref[8], l0, l1, own_ref[30], own_ref[31], r0, r1, high_ref[15])
    for i in range(5):
        for e, tile in enumerate(sources):
            coef[i, e:e + 1, :] = tile[i:i + 1, :]

    lane = lax.broadcasted_iota(jnp.int32, (8, 128), 1)
    order = ((az * 128 + lane) // 2).astype(jnp.float32)
    ratio = order * (1.0 / ORDERS)
    mask = jnp.where(order < coef[4], 1.0, 0.0)
    is_even = lane % 2 == 0
    stiff = coef[0] * mask
    hoop = coef[1] * mask * ratio * ratio
    couple = coef[2] * mask * ratio
    couple_even = jnp.where(is_even, couple, 0.0)
    couple_odd = jnp.where(is_even, 0.0, -couple)
    density = coef[3]
    present = density > 0.0
    inner = jnp.where(present, step_scale / jnp.where(present, density, 1.0), 0.0)
    shared_density = density + pltpu.roll(density, 1, 0)
    edge = jnp.where(present, step_scale / jnp.where(present, shared_density, 1.0), 0.0)
    field[0], field[1], field[2], field[3], field[4], field[5] = (
        stiff, hoop, couple_even, couple_odd, inner, edge)

    for i in range(15):
        for b in range(5):
            u = ucol[i, pl.ds(4 + b, 8, stride=4), :]
            state[0, i, b] = u
            if b < 4:
                state[1, i, b] = u - vcol[i, pl.ds(4 + b, 8, stride=4), :]

    rows = stiffness_rows()

    def one_step(n, carry):
        now = lax.rem(n, 2)
        other = 1 - now
        stiff, hoop = field[0], field[1]
        couple_even, couple_odd = field[2], field[3]
        inner, edge = field[4], field[5]

        def coupled(x):
            return pltpu.roll(x, 127, 1) * couple_even + pltpu.roll(x, 1, 1) * couple_odd

        for s in range(3):
            u = [[state[now, 5 * s + a, b] for b in range(5)] for a in range(5)]
            for a in range(5):
                forces = []
                for b in range(5):
                    total = u[a][b] * float(rows[a, a] + rows[b, b])
                    for other_a in range(5):
                        if other_a != a:
                            total = total + u[other_a][b] * float(rows[a, other_a])
                    for other_b in range(5):
                        if other_b != b:
                            total = total + u[a][other_b] * float(rows[b, other_b])
                    force = -(stiff * total + hoop * u[a][b])
                    if s == 0:
                        force = force + coupled(state[now, 10 + a, b])
                    if s == 2:
                        force = force - coupled(state[now, a, b])
                    forces.append(force)
                forces[0] = forces[0] + pltpu.roll(forces[4], 1, 0)
                for b in range(4):
                    following = (
                        2.0 * u[a][b] - state[other, 5 * s + a, b]
                        + (edge if b == 0 else inner) * forces[b]
                    )
                    state[other, 5 * s + a, b] = following
                    if b == 0:
                        state[other, 5 * s + a, 4] = pltpu.roll(following, 7, 0)
        return carry

    lax.fori_loop(0, STEPS, one_step, 0)
    last = STEPS % 2
    for i in range(15):
        for b in range(4):
            ucol[i, pl.ds(4 + b, 8, stride=4), :] = state[last, i, b]
    for q in range(4):
        gather_ref[q, 15:17] = jnp.zeros((2, 8, 128), jnp.float32)
    for i in range(15):
        own = ucol[i, 16:24, :]
        rim = ucol[i, 24:25, :]
        u_ref[i] = own
        for q in range(4):
            gather_ref[q, i] = own
            gather_ref[q, 15 + i // 8, i % 8:i % 8 + 1, :] = rim


def march(place, own, sib, cross, low, high):
    f32 = jnp.float32
    vmem = pl.BlockSpec(memory_space=pltpu.VMEM)
    return pl.pallas_call(
        step_kernel,
        in_specs=[pl.BlockSpec(memory_space=pltpu.SMEM)] + [vmem] * 5,
        out_specs=(vmem, vmem),
        out_shape=(
            jax.ShapeDtypeStruct((15, 8, 128), f32),
            jax.ShapeDtypeStruct((4, 17, 8, 128), f32),
        ),
        scratch_shapes=[
            pltpu.VMEM((15, 40, 128), f32),
            pltpu.VMEM((15, 40, 128), f32),
            pltpu.VMEM((5, 8, 128), f32),
            pltpu.VMEM((2, 15, 5, 8, 128), f32),
            pltpu.VMEM((6, 8, 128), f32),
        ],
        name="march",
    )(place, own, sib, cross, low, high)


def weight_kernel(table_ref, owners_ref, lanes_ref, value_ref, pair_ref, last_ref, extra_ref):
    table = table_ref[...]
    xi, eta, second, scale = table[:, 0:1], table[:, 1:2], table[:, 2:3], table[:, 3:4]
    owner, code = table[:, 4:5], table[:, 5:6]

    def basis(x, rows):
        d1, d2, d3, d4 = x - rows[0], x - rows[1], x - rows[2], x - rows[3]
        d12, d34 = d1 * d2, d3 * d4
        return d12 * d34 * rows[4], ((d1 + d2) * d34 + d12 * (d3 + d4)) * rows[4]

    lanes = [lanes_ref[i:i + 1, :] for i in range(16)]
    value_a, slope_a = basis(xi, lanes[0:5])
    first_b = basis(eta, lanes[5:10])
    second_b = basis(eta, lanes[10:15])
    value_b = jnp.where(second > 0.5, second_b[0], first_b[0])
    slope_b = jnp.where(second > 0.5, second_b[1], first_b[1])
    along = split(jnp.concatenate([slope_a * value_b, value_a * slope_b], axis=0))
    around = split(value_a * value_b * scale)

    owners = owners_ref[0:1, :]
    lane = lax.broadcasted_iota(jnp.int32, (64, 128), 1)
    earlier = lax.broadcasted_iota(jnp.int32, (64, 128), 0) < lane % 64
    rank = jnp.sum(jnp.where((owner == owners) & earlier, 1.0, 0.0), axis=0, keepdims=True)
    slot = owners * 2.0 + rank

    row = lax.broadcasted_iota(jnp.int32, (512, 128), 0)
    column = lax.broadcasted_iota(jnp.int32, (512, 128), 1)
    half = (row // 4) % 2
    row_slot = (row // 8) * 4 + row % 4
    hit = slot == row_slot.astype(jnp.float32)
    in_half = (column // 64) == half
    value_place = jnp.where(hit & in_half, 1.0, 0.0).astype(jnp.bfloat16)
    around_place = jnp.where(hit & (column < 64), 1.0, 0.0).astype(jnp.bfloat16)
    for n in range(2):
        value_ref[n] = dot(value_place, along[n]).astype(jnp.bfloat16)
    row2 = lax.broadcasted_iota(jnp.int32, (512, 256), 0)
    half2 = ((row2 // 4) % 2).astype(jnp.float32)
    component = lanes[15]
    pad = jnp.zeros((64, 256), jnp.bfloat16)
    for n in range(2):
        weights = dot(around_place, jnp.concatenate([around[n], pad], axis=0))
        pair_ref[n] = jnp.where(component == half2 + 1.0, weights, 0.0).astype(jnp.bfloat16)
        last_ref[n] = jnp.where((component == 3.0) & (half2 == 0.0), weights, 0.0).astype(jnp.bfloat16)
    codes = jnp.concatenate(
        [jnp.broadcast_to(code, (64, 128)), jnp.zeros((64, 128), jnp.float32)], axis=0
    ).astype(jnp.bfloat16)
    extra_ref[...] = jnp.where(half == 1, dot(around_place, codes), 0.0)


def point_weights(table, owners, lanes):
    bf16 = jnp.bfloat16
    return pl.pallas_call(
        weight_kernel,
        out_shape=(
            jax.ShapeDtypeStruct((2, 512, 256), bf16),
            jax.ShapeDtypeStruct((2, 512, 256), bf16),
            jax.ShapeDtypeStruct((2, 512, 256), bf16),
            jax.ShapeDtypeStruct((512, 128), jnp.float32),
        ),
        name="weights",
    )(table, owners, lanes)


def message_kernel(nodes_ref, basis_ref, value_ref, pair_ref, last_ref, extra_ref, out_ref):
    coefs = jnp.concatenate([nodes_ref[q].reshape(136, 128) for q in range(4)], axis=1)
    high, low = split(coefs)
    samples = dot(high, basis_ref[0]) + (dot(low, basis_ref[0]) + dot(high, basis_ref[1]))
    row = lax.broadcasted_iota(jnp.int32, (136, 128), 0)
    component = jnp.where(row < 120, row // 40, (row - 120) // 5)
    values, slopes = samples[:, :128], samples[:, 128:]
    pad = jnp.zeros((120, 384), jnp.float32)
    spread = jnp.concatenate([jnp.where(component == s, values, 0.0) for s in range(3)], axis=1)
    high, low = split(jnp.concatenate([spread, pad], axis=0))
    along = dot(value_ref[0], high) + (dot(value_ref[1], high) + dot(value_ref[0], low))
    for s in range(3):
        out_ref[:, s] = along[:, 128 * s:128 * s + 128].reshape(64, 8, 128)
    high, low = split(jnp.concatenate([slopes, pad[:, :128]], axis=0))
    pair = dot(pair_ref[0], high) + (dot(pair_ref[1], high) + dot(pair_ref[0], low))
    out_ref[:, 3] = pair.reshape(64, 8, 128)
    last = dot(last_ref[0], high) + (dot(last_ref[1], high) + dot(last_ref[0], low))
    out_ref[:, 4] = (last + extra_ref[...]).reshape(64, 8, 128)


def messages(nodes, basis, value, pair, last, extra):
    return pl.pallas_call(
        message_kernel,
        out_shape=jax.ShapeDtypeStruct((64, 5, 8, 128), jnp.float32),
        name="messages",
    )(nodes, basis, value, pair, last, extra)


def voxel_kernel(place_ref, arrived_ref, own_ref, sib_ref, out_ref):
    is_low = place_ref[0] == 0
    tail = arrived_ref[:, 4]
    sub = lax.broadcasted_iota(jnp.int32, (64, 8, 128), 1)
    codes = jnp.where(sub >= 4, tail, pltpu.roll(tail, 4, 1)).reshape(512, 128)
    row = lax.broadcasted_iota(jnp.int32, (512, 128), 0)
    lane = lax.broadcasted_iota(jnp.int32, (512, 128), 1)
    match = ((row // 2) % 4 == lane // 32) & (codes == (lane % 32 + 1).astype(jnp.float32))
    sorting = jnp.where(match, 1.0, 0.0).astype(jnp.bfloat16)
    which = ((0, 1), (3, 4), (6, 7), (2, 5), (8, None))
    totals = [jnp.zeros((32, 128), jnp.float32) for _ in range(2)]
    for t in range(5):
        high, low = split(arrived_ref[:, t].reshape(512, 128))
        both = lax.dot_general(
            sorting, jnp.concatenate([high, low], axis=1), (((0,), (0,)), ((), ())),
            preferred_element_type=jnp.float32,
        )
        summed = both[:, :128] + both[:, 128:]
        for half in range(2):
            g = which[t][half]
            if g is None:
                continue
            for core in range(2):
                mine, theirs = own_ref[g], sib_ref[g]
                adjoint = jnp.where(is_low, mine, theirs) if core == 0 else jnp.where(is_low, theirs, mine)
                first = half * 64 + core * 32
                totals[core] = totals[core] + summed[first:first + 32] * adjoint
    out_ref[0] = totals[0]
    out_ref[1] = totals[1]


def voxels(place, arrived, own, sib):
    vmem = pl.BlockSpec(memory_space=pltpu.VMEM)
    return pl.pallas_call(
        voxel_kernel,
        in_specs=[pl.BlockSpec(memory_space=pltpu.SMEM), vmem, vmem, vmem],
        out_specs=vmem,
        out_shape=jax.ShapeDtypeStruct((2, 32, 128), jnp.float32),
        name="voxels",
    )(place, arrived, own, sib)


def total_kernel(place_ref, mine_ref, theirs_ref, own_ref, inner_ref, edge_ref, full):
    is_low = place_ref[0] == 0
    low = mine_ref[0] + theirs_ref[0]
    high = mine_ref[1] + theirs_ref[1]
    own_ref[...] = jnp.where(is_low, low, high)
    full[0] = low
    full[1] = high
    low_first, low_last = full[0, pl.ds(0, 8, stride=4), :], full[0, pl.ds(3, 8, stride=4), :]
    high_first, high_last = full[1, pl.ds(0, 8, stride=4), :], full[1, pl.ds(3, 8, stride=4), :]
    edge_ref[...] = jnp.where(is_low, low_first, high_last)
    inner_ref[...] = jnp.where(is_low, high_first, low_last)


def total(place, mine, theirs):
    vmem = pl.BlockSpec(memory_space=pltpu.VMEM)
    f32 = jnp.float32
    return pl.pallas_call(
        total_kernel,
        in_specs=[pl.BlockSpec(memory_space=pltpu.SMEM), vmem, vmem],
        out_specs=(vmem, vmem, vmem),
        out_shape=(
            jax.ShapeDtypeStruct((32, 128), f32),
            jax.ShapeDtypeStruct((8, 128), f32),
            jax.ShapeDtypeStruct((8, 128), f32),
        ),
        scratch_shapes=[pltpu.VMEM((2, 32, 128), f32)],
        name="total",
    )(place, mine, theirs)


def smooth_kernel(place_ref, raw_ref, inner_ref, outer_ref, before_ref, after_ref, out_ref, framed):
    is_low = place_ref[0] == 0
    raw = raw_ref[...]
    inner, outer = inner_ref[...], outer_ref[...]
    below = jnp.where(is_low, outer, inner)
    above = jnp.where(is_low, inner, outer)
    framed[0:8] = jnp.zeros((8, 128), jnp.float32)
    framed[8:40] = raw
    framed[40:48] = jnp.zeros((8, 128), jnp.float32)
    lane = lax.broadcasted_iota(jnp.int32, (32, 128), 1)
    row = lax.broadcasted_iota(jnp.int32, (32, 128), 0)
    west = pltpu.roll(jnp.where(lane == 127, before_ref[...], raw), 1, 1)
    east = pltpu.roll(jnp.where(lane == 0, after_ref[...], raw), 127, 1)
    neighbours = framed[4:36] + framed[12:44] + west + east
    down = jnp.where(row % 4 == 0, 0.0, framed[7:39])
    up = jnp.where(row % 4 == 3, 0.0, framed[9:41])
    neighbours = neighbours + down + up
    out_ref[...] = raw + smooth_rate * (neighbours - 6.0 * raw)
    out_ref[pl.ds(0, 8, stride=4), :] += smooth_rate * below
    out_ref[pl.ds(3, 8, stride=4), :] += smooth_rate * above


def smooth(place, raw, inner, outer, before, after):
    vmem = pl.BlockSpec(memory_space=pltpu.VMEM)
    return pl.pallas_call(
        smooth_kernel,
        in_specs=[pl.BlockSpec(memory_space=pltpu.SMEM)] + [vmem] * 5,
        out_specs=vmem,
        out_shape=jax.ShapeDtypeStruct((32, 128), jnp.float32),
        scratch_shapes=[pltpu.VMEM((48, 128), jnp.float32)],
        name="smooth",
    )(place, raw, inner, outer, before, after)


def on_device(
    displacement,
    velocity,
    modulus,
    hoop_strength,
    coupling,
    density,
    order_count,
    point_element,
    point_local,
    azimuth_scale,
    point_owner,
    point_cell,
    adjoint_strain,
):
    f32 = jnp.float32
    count = lax.axis_size(MER)
    az_count = lax.axis_size("az")
    core, az = lax.axis_index("mer_2"), lax.axis_index("az")
    place = jnp.stack([core, az]).astype(jnp.int32)
    swap = [(0, 1), (1, 0)]
    cross = [(c, c + 1) for c in range(1, count - 1, 2)] + [(c + 1, c) for c in range(1, count - 1, 2)]

    own, up, down = pack(
        displacement.reshape(15, 8, 128), velocity.reshape(15, 8, 128),
        modulus, hoop_strength, coupling, density, order_count,
    )
    sib = lax.ppermute(own, "mer_2", swap)
    outer = lax.ppermute(own, MER, cross)
    low = lax.ppermute(up, MER, [(i, i + 2) for i in range(count - 2)])
    high = lax.ppermute(down, MER, [(i + 2, i) for i in range(count - 2)])
    final, spread = march(place, own, sib, outer, low, high)

    owner = point_owner.astype(f32)
    table = jnp.concatenate(
        [
            point_local,
            (point_element[:, 1:2] % 2).astype(f32),
            azimuth_scale[:, None],
            owner,
            (point_cell[:, None] + 1).astype(f32),
            jnp.zeros((64, 2), f32),
        ],
        axis=1,
    )
    owners = jnp.concatenate([owner, owner], axis=0).reshape(1, 128)
    weights = point_weights(table, owners, jnp.asarray(lane_tables()))
    basis = lax.dynamic_index_in_dim(jnp.asarray(basis_tables(az_count)), az, 0, keepdims=False)

    nodes = lax.all_to_all(spread, "az", 0, 0, tiled=True)
    outgoing = messages(nodes, basis, *weights)
    arrived = lax.all_to_all(outgoing, SIDES, 0, 0, tiled=True)

    adjoint = adjoint_strain.reshape(9, 32, 128)
    adjoint_sib = lax.ppermute(adjoint, "mer_2", swap)
    part = voxels(place, arrived, adjoint, adjoint_sib)
    raw, inner, edge = total(place, part, lax.ppermute(part, "mer_2", swap))
    beyond = lax.ppermute(edge, MER, cross)
    ahead = [(i, (i + 1) % az_count) for i in range(az_count)]
    before = lax.ppermute(raw, "az", ahead)
    after = lax.ppermute(raw, "az", [(b, a) for a, b in ahead])
    kernel = smooth(place, raw, inner, beyond, before, after)
    return final.reshape(3, 5, 8, 128), kernel.reshape(8, 4, 128)


def solution(mesh):
    torus = Mesh(mesh.devices.reshape(8, 8, 2, mesh.shape["az"]), ("mer_0", "mer_1", "mer_2", "az"))
    return jax.shard_map(
        on_device,
        mesh=torus,
        in_specs=(
            P(None, None, MER, "az"),
            P(None, None, MER, "az"),
            P(None, MER),
            P(None, MER),
            P(None, MER),
            P(None, MER),
            P(None, MER),
            P(MER, None),
            P(MER, None),
            P(MER),
            P(MER, None),
            P(MER),
            P(None, None, MER, "az"),
        ),
        out_specs=(P(None, None, MER, "az"), P(None, MER, "az")),
        check_vma=False,
    )
```

```python
import math

import jax
import jax.numpy as jnp
import numpy as np
from jax import lax
from jax.experimental import pallas as pl
from jax.experimental.pallas import tpu as pltpu
from jax.sharding import Mesh
from jax.sharding import PartitionSpec as P

ORDERS = 256
STEPS = 3
MER = ("mer_0", "mer_1", "mer_2")
SIDES = ("mer_0", "mer_1")

GRANT = pltpu.CompilerParams(vmem_limit_bytes=16 << 20)

step_scale = 0.015
smooth_rate = 0.125


def gll_tables():
    nodes = np.array([-1.0, -math.sqrt(3.0 / 7.0), 0.0, math.sqrt(3.0 / 7.0), 1.0])
    weights = np.array([0.1, 49.0 / 90.0, 32.0 / 45.0, 49.0 / 90.0, 0.1])
    derivative = np.zeros((5, 5))
    for i in range(5):
        for j in range(5):
            if i == j:
                derivative[i, j] = sum(1.0 / (nodes[i] - nodes[l]) for l in range(5) if l != i)
            else:
                scale_i = np.prod([nodes[i] - nodes[l] for l in range(5) if l != i])
                scale_j = np.prod([nodes[j] - nodes[l] for l in range(5) if l != j])
                derivative[i, j] = scale_i / (scale_j * (nodes[i] - nodes[j]))
    return nodes, weights, derivative


def stiffness_rows():
    _, weights, derivative = gll_tables()
    return (derivative.T @ np.diag(weights) @ derivative) / weights[:, None]


ROWS = 37


def basis_tables():
    k = np.arange(2 * ORDERS)
    order = k // 2
    j = np.zeros(256, np.int64)
    j[:128] = np.arange(128)
    edge = np.arange(128) % 32
    j[128:] = np.where(edge < 9, -1, np.where(edge < 18, 128, 0))
    angle = (order[:, None] * j[None, :] % (2 * ORDERS)) * (2.0 * math.pi / (2 * ORDERS))
    even = (k % 2 == 0)[:, None]
    value = np.where(even, np.cos(angle), np.sin(angle))
    slope = np.where(even, -np.sin(angle), np.cos(angle))
    return (np.stack([value, slope]) / math.sqrt(ORDERS)).astype(np.float32)


def lane_tables():
    nodes = gll_tables()[0]
    rows = np.zeros((16, 256), np.float32)
    for r in range(135):
        if r < 120:
            s, a, c = r // 40, r // 8 % 5, r % 8
        else:
            s, a, c = (r - 120) // 5, (r - 120) % 5, 8

        def place(first, n):
            others = [l for l in range(5) if l != n]
            for i, l in enumerate(others):
                rows[first + i, r] = nodes[l]
            rows[first + 4, r] = 1.0 / np.prod([nodes[n] - nodes[l] for l in others])

        place(0, a)
        if c <= 4:
            place(5, c)
        if c >= 4:
            place(10, c - 4)
        rows[15, r] = s + 1
    return rows


def constant_table():
    return np.concatenate([basis_tables().reshape(1024, 256), lane_tables()], axis=0)


def split(x):
    high = x.astype(jnp.bfloat16)
    low = (x - high.astype(jnp.float32)).astype(jnp.bfloat16)
    return high, low


def dot(a, b):
    return jnp.dot(a, b, preferred_element_type=jnp.float32)


def fetch(pairs, arrived):
    copies = [pltpu.make_async_copy(a, b, arrived.at[i]) for i, (a, b) in enumerate(pairs)]
    for copy in copies:
        copy.start()
    return copies


def pack_kernel(*refs):
    sources, (own_ref, up_ref, down_ref, points_ref) = refs[:12], refs[12:16]
    scratch, arrived = refs[16:28], refs[28]
    copies = fetch(list(zip(sources, scratch)), arrived)
    u_ref, v_ref = scratch[:2]
    element_ref, local_ref, scale_ref, owner_ref, cell_ref = scratch[7:]
    f32 = jnp.float32
    own_ref[30:32] = jnp.zeros((2, 8, 128), f32)
    up_ref[7] = jnp.zeros((8, 128), f32)
    up_ref[8] = jnp.zeros((8, 128), f32)
    down_ref[15] = jnp.zeros((8, 128), f32)
    points_ref[...] = jnp.zeros((8, 128), f32)
    for copy in copies:
        copy.wait()
    for i in range(15):
        u, v = u_ref[i], v_ref[i]
        own_ref[i] = u
        own_ref[15 + i] = v
        up_ref[i // 2, 4 * (i % 2):4 * (i % 2) + 4, :] = u_ref[i, 4:8, :]
        down_ref[i] = u
        down_ref[i, 5:6, :] = v_ref[i, 0:1, :]
    for i, ref in enumerate(scratch[2:7]):
        both = ref[...].astype(f32)
        first = jnp.broadcast_to(both[:, 0:1], (1, 128))
        second = jnp.broadcast_to(both[:, 1:2], (1, 128))
        own_ref[30, i:i + 1, :] = first
        own_ref[31, i:i + 1, :] = second
        down_ref[15, i:i + 1, :] = first
        up_ref[8, i:i + 1, :] = second
    points_ref[0:2, 0:64] = local_ref[...]
    points_ref[2:3, 0:64] = (element_ref[1:2, :] % 2).astype(f32)
    points_ref[3:4, 0:64] = scale_ref[...]
    points_ref[4:5, 0:64] = owner_ref[...].astype(f32)
    points_ref[5:6, 0:64] = (cell_ref[...] + 1).astype(f32)


def pack(*arrays):
    f32 = jnp.float32
    hbm, vmem = pl.BlockSpec(memory_space=pltpu.HBM), pl.BlockSpec(memory_space=pltpu.VMEM)
    return pl.pallas_call(
        pack_kernel,
        in_specs=[hbm] * 12,
        out_specs=(vmem, vmem, vmem, vmem),
        scratch_shapes=[pltpu.VMEM(a.shape, a.dtype) for a in arrays] + [pltpu.SemaphoreType.DMA((12,))],
        out_shape=(
            jax.ShapeDtypeStruct((32, 8, 128), f32),
            jax.ShapeDtypeStruct((9, 8, 128), f32),
            jax.ShapeDtypeStruct((16, 8, 128), f32),
            jax.ShapeDtypeStruct((8, 128), f32),
        ),
        name="pack",
    )(*arrays)


def step_kernel(own_ref, sib_ref, cross_ref, low_ref, high_ref, u_ref, gather_ref,
                ucol, vcol, coef, state, field):
    core, az = lax.axis_index("mer_2"), lax.axis_index("az")
    is_low = core == 0

    def left(i):
        return jnp.where(is_low, cross_ref[i], sib_ref[i])

    def right(i):
        return jnp.where(is_low, sib_ref[i], cross_ref[i])

    zero4 = jnp.zeros((4, 128), jnp.float32)
    zero8 = jnp.zeros((8, 128), jnp.float32)
    for i in range(15):
        ucol[i, 0:8, :] = zero8
        ucol[i, 4:8, :] = low_ref[i // 2, 4 * (i % 2):4 * (i % 2) + 4, :]
        ucol[i, 8:16, :] = left(i)
        ucol[i, 16:24, :] = own_ref[i]
        ucol[i, 24:32, :] = right(i)
        ucol[i, 32:40, :] = high_ref[i]
        vcol[i, 0:8, :] = zero8
        vcol[i, 8:16, :] = left(15 + i)
        vcol[i, 16:24, :] = own_ref[15 + i]
        vcol[i, 24:32, :] = right(15 + i)
        vcol[i, 32:40, :] = zero8
        vcol[i, 32:33, :] = high_ref[i, 5:6, :]
    l0, l1, r0, r1 = left(30), left(31), right(30), right(31)
    sources = (low_ref[8], l0, l1, own_ref[30], own_ref[31], r0, r1, high_ref[15])
    for i in range(5):
        for e, tile in enumerate(sources):
            coef[i, e:e + 1, :] = tile[i:i + 1, :]

    lane = lax.broadcasted_iota(jnp.int32, (8, 128), 1)
    order = ((az * 128 + lane) // 2).astype(jnp.float32)
    ratio = order * (1.0 / ORDERS)
    mask = jnp.where(order < coef[4], 1.0, 0.0)
    is_even = lane % 2 == 0
    stiff = coef[0] * mask
    hoop = coef[1] * mask * ratio * ratio
    couple = coef[2] * mask * ratio
    couple_even = jnp.where(is_even, couple, 0.0)
    couple_odd = jnp.where(is_even, 0.0, -couple)
    density = coef[3]
    present = density > 0.0
    inner = jnp.where(present, step_scale / jnp.where(present, density, 1.0), 0.0)
    shared_density = density + pltpu.roll(density, 1, 0)
    edge = jnp.where(present, step_scale / jnp.where(present, shared_density, 1.0), 0.0)
    field[0], field[1], field[2], field[3], field[4], field[5] = (
        stiff, hoop, couple_even, couple_odd, inner, edge)

    for i in range(15):
        for b in range(5):
            u = ucol[i, pl.ds(4 + b, 8, stride=4), :]
            state[0, i, b] = u
            if b < 4:
                state[1, i, b] = u - vcol[i, pl.ds(4 + b, 8, stride=4), :]

    rows = stiffness_rows()

    def one_step(n, carry):
        now = lax.rem(n, 2)
        other = 1 - now
        stiff, hoop = field[0], field[1]
        couple_even, couple_odd = field[2], field[3]
        inner, edge = field[4], field[5]

        def coupled(x):
            return pltpu.roll(x, 127, 1) * couple_even + pltpu.roll(x, 1, 1) * couple_odd

        for s in range(3):
            u = [[state[now, 5 * s + a, b] for b in range(5)] for a in range(5)]
            for a in range(5):
                forces = []
                for b in range(5):
                    total = u[a][b] * float(rows[a, a] + rows[b, b])
                    for other_a in range(5):
                        if other_a != a:
                            total = total + u[other_a][b] * float(rows[a, other_a])
                    for other_b in range(5):
                        if other_b != b:
                            total = total + u[a][other_b] * float(rows[b, other_b])
                    force = -(stiff * total + hoop * u[a][b])
                    if s == 0:
                        force = force + coupled(state[now, 10 + a, b])
                    if s == 2:
                        force = force - coupled(state[now, a, b])
                    forces.append(force)
                forces[0] = forces[0] + pltpu.roll(forces[4], 1, 0)
                for b in range(4):
                    following = (
                        2.0 * u[a][b] - state[other, 5 * s + a, b]
                        + (edge if b == 0 else inner) * forces[b]
                    )
                    state[other, 5 * s + a, b] = following
                    if b == 0:
                        state[other, 5 * s + a, 4] = pltpu.roll(following, 7, 0)
        return carry

    lax.fori_loop(0, STEPS, one_step, 0)
    last = STEPS % 2
    for i in range(15):
        for b in range(4):
            ucol[i, pl.ds(4 + b, 8, stride=4), :] = state[last, i, b]
    for q in range(4):
        gather_ref[q, 15:17] = jnp.zeros((2, 8, 128), jnp.float32)
    for i in range(15):
        own = ucol[i, 16:24, :]
        rim = ucol[i, 24:25, :]
        u_ref[i] = own
        for q in range(4):
            gather_ref[q, i] = own
            gather_ref[q, 15 + i // 8, i % 8:i % 8 + 1, :] = rim


def march(own, sib, cross, low, high):
    f32 = jnp.float32
    vmem = pl.BlockSpec(memory_space=pltpu.VMEM)
    return pl.pallas_call(
        step_kernel,
        in_specs=[vmem] * 5,
        out_specs=(vmem, vmem),
        out_shape=(
            jax.ShapeDtypeStruct((15, 8, 128), f32),
            jax.ShapeDtypeStruct((4, 17, 8, 128), f32),
        ),
        scratch_shapes=[
            pltpu.VMEM((15, 40, 128), f32),
            pltpu.VMEM((15, 40, 128), f32),
            pltpu.VMEM((5, 8, 128), f32),
            pltpu.VMEM((2, 15, 5, 8, 128), f32),
            pltpu.VMEM((6, 8, 128), f32),
        ],
        compiler_params=GRANT,
        name="march",
    )(own, sib, cross, low, high)


def weight_kernel(points_ref, table_ref, weight_ref, point_ref, basis_ref):
    f32, bf16 = jnp.float32, jnp.bfloat16
    az = lax.axis_index("az")
    diagonal = (lax.broadcasted_iota(jnp.int32, (64, 128), 0)
                == lax.broadcasted_iota(jnp.int32, (64, 128), 1))

    def upright(line):
        return jnp.sum(jnp.where(diagonal, line, 0.0), axis=1, keepdims=True)

    xi, eta, second, scale, owner, code = (upright(points_ref[i:i + 1, :]) for i in range(6))

    def basis(x, rows):
        d1, d2, d3, d4 = x - rows[0], x - rows[1], x - rows[2], x - rows[3]
        d12, d34 = d1 * d2, d3 * d4
        return d12 * d34 * rows[4], ((d1 + d2) * d34 + d12 * (d3 + d4)) * rows[4]

    lanes = [table_ref[1024 + i:1025 + i, :] for i in range(16)]
    value_a, slope_a = basis(xi, lanes[0:5])
    first_b = basis(eta, lanes[5:10])
    second_b = basis(eta, lanes[10:15])
    value_b = jnp.where(second > 0.5, second_b[0], first_b[0])
    slope_b = jnp.where(second > 0.5, second_b[1], first_b[1])
    around = value_a * value_b * scale
    point = split(jnp.concatenate([slope_a * value_b, value_a * slope_b, around], axis=0))
    point_ref[0, 0:192] = point[0]
    point_ref[1, 0:192] = point[1]

    lane = lax.broadcasted_iota(jnp.int32, (64, 128), 1)
    sub = lax.broadcasted_iota(jnp.int32, (64, 128), 0)
    owners = points_ref[4:5, :]
    rank = jnp.sum(jnp.where((owner == owners) & (sub < lane), 1.0, 0.0), axis=0, keepdims=True)
    slot = owners * 2.0 + rank
    row = lax.broadcasted_iota(jnp.int32, (256, 128), 0)
    column = lax.broadcasted_iota(jnp.int32, (256, 128), 1)
    row_slot = (row % 64) * 4 + row // 64
    place = jnp.where((slot == row_slot.astype(f32)) & (column < 64), 1.0, 0.0).astype(bf16)[:, :64]
    for n in range(2):
        for d in range(3):
            weight_ref[2 * d + n] = dot(place, point[n][64 * d:64 * d + 64]).astype(bf16)

    upright_slot = upright(slot)
    group = (lane // 32).astype(f32)
    mine = upright_slot - 4.0 * jnp.floor(upright_slot * 0.25) == group
    point_ref[0, 192:256, 0:128] = jnp.where(mine & (lane % 32 == 31), code, 0.0).astype(bf16)
    point_ref[0, 192:256, 128:256] = jnp.where(mine & (lane % 32 < 18), 1.0, 0.0).astype(bf16)
    chip = jnp.where((jnp.floor(slot * 0.25) == sub.astype(f32)) & (lane < 64), 1.0, 0.0).astype(bf16)
    point_ref[1, 192:256, 0:128] = chip
    point_ref[1, 192:256, 128:256] = chip

    order = lax.broadcasted_iota(jnp.int32, (512, 128), 0) // 2
    turns = (order * az) % 4
    along = jnp.where(turns == 0, 1.0, jnp.where(turns == 2, -1.0, 0.0))
    across = jnp.where(turns == 1, 1.0, jnp.where(turns == 3, -1.0, 0.0))
    ratio = order.astype(f32) * (1.0 / ORDERS)
    first, other = slice(0, 512), slice(512, 1024)
    low_lanes, edge_lanes = slice(0, 128), slice(128, 256)
    value = along * table_ref[first, low_lanes] + across * table_ref[other, low_lanes]
    slope = ratio * (along * table_ref[other, low_lanes] - across * table_ref[first, low_lanes])
    edge_value = along * table_ref[first, edge_lanes] + across * table_ref[other, edge_lanes]
    edge_slope = ratio * (along * table_ref[other, edge_lanes] - across * table_ref[first, edge_lanes])
    kind = ((lax.broadcasted_iota(jnp.int32, (512, 128), 1) % 32) % 9) % 3
    edge = jnp.where(kind == 2, edge_slope, edge_value)
    for i, block in enumerate((value, slope, edge)):
        high, low = split(block)
        basis_ref[0, :, 128 * i:128 * i + 128] = high
        basis_ref[1, :, 128 * i:128 * i + 128] = low


def point_weights(points):
    bf16 = jnp.bfloat16
    return pl.pallas_call(
        weight_kernel,
        out_shape=(
            jax.ShapeDtypeStruct((6, 256, 256), bf16),
            jax.ShapeDtypeStruct((2, 256, 256), bf16),
            jax.ShapeDtypeStruct((2, 512, 384), bf16),
        ),
        compiler_params=GRANT,
        name="weights",
    )(points, jnp.asarray(constant_table()))


def thrice(a, b):
    return dot(a[0], b[0]) + (dot(a[1], b[0]) + dot(a[0], b[1]))


def message_kernel(nodes_ref, weight_ref, point_ref, basis_ref, out_ref):
    f32 = jnp.float32
    coefs = jnp.concatenate([nodes_ref[q].reshape(136, 128) for q in range(4)], axis=1)
    samples = thrice(split(coefs), (basis_ref[0], basis_ref[1]))
    row = lax.broadcasted_iota(jnp.int32, (136, 128), 0)
    component = jnp.where(row < 120, row // 40, (row - 120) // 5)
    pad = jnp.zeros((120, 384), f32)
    values, slopes, edges = samples[:, :128], samples[:, 128:256], samples[:, 256:]

    def spread(block):
        parts = jnp.concatenate([jnp.where(component == s, block, 0.0) for s in range(3)], axis=1)
        return split(jnp.concatenate([parts, pad], axis=0))

    by_kind = (spread(values), None, spread(slopes))
    for d in range(3):
        field = by_kind[0] if d < 2 else by_kind[2]
        rows = thrice((weight_ref[2 * d], weight_ref[2 * d + 1]), field)
        for s in range(3):
            for c in range(4):
                out_ref[pl.ds(4 * (3 * s + d) + c, 64, stride=ROWS), :] = (
                    rows[64 * c:64 * c + 64, 128 * s:128 * s + 128])

    lane = lax.broadcasted_iota(jnp.int32, (136, 128), 1)
    edges = jnp.where(((lane % 32) % 9) // 3 == component, edges, 0.0)
    edges = split(jnp.concatenate([edges, pad[:, :128]], axis=0))
    rows = thrice((point_ref[0, 0:192], point_ref[1, 0:192]), edges)
    lane = lax.broadcasted_iota(jnp.int32, (64, 128), 1)
    kind = ((lane % 32) % 9) % 3
    extra = jnp.where(kind == 0, rows[:64], jnp.where(kind == 1, rows[64:128], rows[128:]))
    extra = (extra * point_ref[0, 192:256, 128:256].astype(f32)
             + point_ref[0, 192:256, 0:128].astype(f32))
    chip = point_ref[1, 192:256, 0:64]
    high, low = split(extra)
    out_ref[pl.ds(36, 64, stride=ROWS), :] = dot(chip, high) + dot(chip, low)


def messages(nodes, *weights):
    return pl.pallas_call(
        message_kernel,
        out_shape=jax.ShapeDtypeStruct((64 * ROWS, 128), jnp.float32),
        compiler_params=GRANT,
        name="messages",
    )(nodes, *weights)


def rims_kernel(own_ref, sib_ref, first_ref, last_ref):
    lane = lax.broadcasted_iota(jnp.int32, (32, 128), 1)
    for n, ref in enumerate((own_ref, sib_ref)):
        first = jnp.zeros((32, 128), jnp.float32)
        last = jnp.zeros((32, 128), jnp.float32)
        for g in range(9):
            first = jnp.where(lane == 9 + g, ref[g, :, 0:1], first)
            last = jnp.where(lane == g, ref[g, :, 127:128], last)
        first_ref[n] = first
        last_ref[n] = last


def rims(own, sib):
    shape = jax.ShapeDtypeStruct((2, 32, 128), jnp.float32)
    return pl.pallas_call(
        rims_kernel, out_shape=(shape, shape), compiler_params=GRANT, name="rims",
    )(own, sib)


def voxel_kernel(arrived_ref, own_ref, sib_ref, before_ref, after_ref, out_ref, cross_ref, diag_ref):
    is_low = lax.axis_index("mer_2") == 0
    f32 = jnp.float32
    tail = arrived_ref[pl.ds(36, 64, stride=ROWS), :]
    lane = lax.broadcasted_iota(jnp.int32, (64, 128), 1)
    wanted = (lane % 32 + 1).astype(f32)
    sorting = jnp.concatenate(
        [
            jnp.where((lane // 32 == c // 2) & (tail[:, 32 * c + 31:32 * c + 32] == wanted), 1.0, 0.0)
            for c in range(4)
        ],
        axis=0,
    ).astype(jnp.bfloat16)

    def sorted_sum(rows):
        high, low = split(rows)
        both = lax.dot_general(
            sorting, jnp.concatenate([high, low], axis=1), (((0,), (0,)), ((), ())),
            preferred_element_type=f32,
        )
        return both[:64, :128] + both[:64, 128:]

    totals = [jnp.zeros((32, 128), f32) for _ in range(2)]
    for g in range(9):
        summed = sorted_sum(jnp.concatenate(
            [arrived_ref[pl.ds(4 * g + c, 64, stride=ROWS), :] for c in range(4)], axis=0))
        mine, theirs = own_ref[g], sib_ref[g]
        totals[0] = totals[0] + summed[:32] * jnp.where(is_low, mine, theirs)
        totals[1] = totals[1] + summed[32:] * jnp.where(is_low, theirs, mine)
    shifted = [tail] + [pltpu.roll(tail, 128 - 32 * c, 1) for c in range(1, 4)]
    ends = sorted_sum(jnp.concatenate([jnp.where(lane < 18, x, 0.0) for x in shifted], axis=0))
    own_edge, sib_edge = before_ref[0] + after_ref[0], before_ref[1] + after_ref[1]
    side = (ends[:32] * jnp.where(is_low, own_edge, sib_edge), ends[32:] * jnp.where(is_low, sib_edge, own_edge))
    out_ref[0] = totals[0]
    out_ref[1] = totals[1]
    for core in range(2):
        product = side[core]
        small = lax.broadcasted_iota(jnp.int32, (32, 128), 1)
        west = jnp.sum(jnp.where(small < 9, product, 0.0), axis=1, keepdims=True)
        east = jnp.sum(jnp.where((small >= 9) & (small < 18), product, 0.0), axis=1, keepdims=True)
        out_ref[2 + core] = jnp.where(small == 127, west, jnp.where(small == 0, east, 0.0))
    bottom = out_ref[0, pl.ds(0, 8, stride=4), :]
    top = out_ref[1, pl.ds(3, 8, stride=4), :]
    cross_ref[...] = jnp.where(is_low, bottom, top)
    diag_ref[...] = jnp.where(is_low, top, bottom)


def voxels(arrived, own, sib, before, after):
    f32 = jnp.float32
    return pl.pallas_call(
        voxel_kernel,
        out_shape=(
            jax.ShapeDtypeStruct((4, 32, 128), f32),
            jax.ShapeDtypeStruct((8, 128), f32),
            jax.ShapeDtypeStruct((8, 128), f32),
        ),
        compiler_params=GRANT,
        name="voxels",
    )(arrived, own, sib, before, after)


def smooth_kernel(mine_ref, theirs_ref, cross_ref, diag_ref, out_ref, full, framed):
    is_low = lax.axis_index("mer_2") == 0
    low = mine_ref[0] + theirs_ref[0]
    high = mine_ref[1] + theirs_ref[1]
    raw = jnp.where(is_low, low, high)
    ends = jnp.where(is_low, mine_ref[2] + theirs_ref[2], mine_ref[3] + theirs_ref[3])
    full[0] = low
    full[1] = high
    outer = cross_ref[...] + diag_ref[...]
    below = jnp.where(is_low, outer, full[0, pl.ds(3, 8, stride=4), :])
    above = jnp.where(is_low, full[1, pl.ds(0, 8, stride=4), :], outer)
    framed[0:8] = jnp.zeros((8, 128), jnp.float32)
    framed[8:40] = raw
    framed[40:48] = jnp.zeros((8, 128), jnp.float32)
    lane = lax.broadcasted_iota(jnp.int32, (32, 128), 1)
    row = lax.broadcasted_iota(jnp.int32, (32, 128), 0)
    west = pltpu.roll(jnp.where(lane == 127, ends, raw), 1, 1)
    east = pltpu.roll(jnp.where(lane == 0, ends, raw), 127, 1)
    neighbours = framed[4:36] + framed[12:44] + west + east
    down = jnp.where(row % 4 == 0, 0.0, framed[7:39])
    up = jnp.where(row % 4 == 3, 0.0, framed[9:41])
    neighbours = neighbours + down + up
    out_ref[...] = raw + smooth_rate * (neighbours - 6.0 * raw)
    out_ref[pl.ds(0, 8, stride=4), :] += smooth_rate * below
    out_ref[pl.ds(3, 8, stride=4), :] += smooth_rate * above


def smooth(mine, theirs, cross, diag):
    return pl.pallas_call(
        smooth_kernel,
        out_shape=jax.ShapeDtypeStruct((32, 128), jnp.float32),
        scratch_shapes=[pltpu.VMEM((2, 32, 128), jnp.float32), pltpu.VMEM((48, 128), jnp.float32)],
        compiler_params=GRANT,
        name="smooth",
    )(mine, theirs, cross, diag)


def on_device(
    displacement,
    velocity,
    modulus,
    hoop_strength,
    coupling,
    density,
    order_count,
    point_element,
    point_local,
    azimuth_scale,
    point_owner,
    point_cell,
    adjoint_strain,
):
    count = lax.axis_size(MER)
    az_count = lax.axis_size("az")
    swap = [(0, 1), (1, 0)]
    cross = [(c, c + 1) for c in range(1, count - 1, 2)] + [(c + 1, c) for c in range(1, count - 1, 2)]
    diagonal = [(c, c + 2) for c in range(0, count - 2, 2)] + [(c + 2, c) for c in range(1, count - 2, 2)]
    ahead = [(i, (i + 1) % az_count) for i in range(az_count)]

    own, up, down, points = pack(
        displacement.reshape(15, 8, 128), velocity.reshape(15, 8, 128),
        modulus, hoop_strength, coupling, density, order_count,
        point_element.T, point_local.T, azimuth_scale.reshape(1, 64), point_owner.reshape(1, 64),
        point_cell.reshape(1, 64),
    )
    sib = lax.ppermute(own, "mer_2", swap)
    outer = lax.ppermute(own, MER, cross)
    low = lax.ppermute(up, MER, [(i, i + 2) for i in range(count - 2)])
    high = lax.ppermute(down, MER, [(i + 2, i) for i in range(count - 2)])
    final, spread = march(own, sib, outer, low, high)

    weights = point_weights(points)
    nodes = lax.all_to_all(spread, "az", 0, 0, tiled=True)
    outgoing = messages(nodes, *weights)
    arrived = lax.all_to_all(outgoing.reshape(64, ROWS, 1, 128), SIDES, 0, 0, tiled=True)
    arrived = arrived.reshape(64 * ROWS, 128)

    adjoint = adjoint_strain.reshape(9, 32, 128)
    adjoint_sib = lax.ppermute(adjoint, "mer_2", swap)
    first, last = rims(adjoint, adjoint_sib)
    before = lax.ppermute(last, "az", ahead)
    after = lax.ppermute(first, "az", [(b, a) for a, b in ahead])
    part, near, far = voxels(arrived, adjoint, adjoint_sib, before, after)
    kernel = smooth(
        part, lax.ppermute(part, "mer_2", swap), lax.ppermute(near, MER, cross), lax.ppermute(far, MER, diagonal)
    )
    return final.reshape(3, 5, 8, 128), kernel.reshape(8, 4, 128)


def solution(mesh):
    torus = Mesh(mesh.devices.reshape(8, 8, 2, mesh.shape["az"]), ("mer_0", "mer_1", "mer_2", "az"))
    return jax.shard_map(
        on_device,
        mesh=torus,
        in_specs=(
            P(None, None, MER, "az"),
            P(None, None, MER, "az"),
            P(None, MER),
            P(None, MER),
            P(None, MER),
            P(None, MER),
            P(None, MER),
            P(MER, None),
            P(MER, None),
            P(MER),
            P(MER, None),
            P(MER),
            P(None, None, MER, "az"),
        ),
        out_specs=(P(None, None, MER, "az"), P(None, MER, "az")),
        check_vma=False,
    )
```

```python
import math

import jax
import jax.numpy as jnp
import numpy as np
from jax import lax
from jax.experimental import pallas as pl
from jax.experimental.pallas import tpu as pltpu
from jax.sharding import Mesh
from jax.sharding import PartitionSpec as P

ORDERS = 256
STEPS = 3
MER = ("mer_0", "mer_1", "mer_2")
SIDES = ("mer_0", "mer_1")

GRANT = pltpu.CompilerParams(vmem_limit_bytes=16 << 20)

step_scale = 0.015
smooth_rate = 0.125


def gll_tables():
    nodes = np.array([-1.0, -math.sqrt(3.0 / 7.0), 0.0, math.sqrt(3.0 / 7.0), 1.0])
    weights = np.array([0.1, 49.0 / 90.0, 32.0 / 45.0, 49.0 / 90.0, 0.1])
    derivative = np.zeros((5, 5))
    for i in range(5):
        for j in range(5):
            if i == j:
                derivative[i, j] = sum(1.0 / (nodes[i] - nodes[l]) for l in range(5) if l != i)
            else:
                scale_i = np.prod([nodes[i] - nodes[l] for l in range(5) if l != i])
                scale_j = np.prod([nodes[j] - nodes[l] for l in range(5) if l != j])
                derivative[i, j] = scale_i / (scale_j * (nodes[i] - nodes[j]))
    return nodes, weights, derivative


def stiffness_rows():
    _, weights, derivative = gll_tables()
    return (derivative.T @ np.diag(weights) @ derivative) / weights[:, None]


ROWS = 37


def basis_tables():
    k = np.arange(2 * ORDERS)
    order = k // 2
    j = np.zeros(256, np.int64)
    j[:128] = np.arange(128)
    edge = np.arange(128) % 32
    j[128:] = np.where(edge < 9, -1, np.where(edge < 18, 128, 0))
    angle = (order[:, None] * j[None, :] % (2 * ORDERS)) * (2.0 * math.pi / (2 * ORDERS))
    even = (k % 2 == 0)[:, None]
    value = np.where(even, np.cos(angle), np.sin(angle))
    slope = np.where(even, -np.sin(angle), np.cos(angle))
    return (np.stack([value, slope]) / math.sqrt(ORDERS)).astype(np.float32)


def lane_tables():
    nodes = gll_tables()[0]
    rows = np.zeros((16, 256), np.float32)
    for r in range(135):
        if r < 120:
            s, a, c = r // 40, r // 8 % 5, r % 8
        else:
            s, a, c = (r - 120) // 5, (r - 120) % 5, 8

        def place(first, n):
            others = [l for l in range(5) if l != n]
            for i, l in enumerate(others):
                rows[first + i, r] = nodes[l]
            rows[first + 4, r] = 1.0 / np.prod([nodes[n] - nodes[l] for l in others])

        place(0, a)
        if c <= 4:
            place(5, c)
        if c >= 4:
            place(10, c - 4)
        rows[15, r] = s + 1
    return rows


def constant_table():
    return np.concatenate([basis_tables().reshape(1024, 256), lane_tables()], axis=0)


def split(x):
    high = x.astype(jnp.bfloat16)
    low = (x - high.astype(jnp.float32)).astype(jnp.bfloat16)
    return high, low


def dot(a, b):
    return jnp.dot(a, b, preferred_element_type=jnp.float32)


def fetch(pairs, arrived):
    copies = [pltpu.make_async_copy(a, b, arrived.at[i]) for i, (a, b) in enumerate(pairs)]
    for copy in copies:
        copy.start()
    return copies


def pack_kernel(*refs):
    sources, (own_ref, points_ref) = refs[:12], refs[12:14]
    scratch, arrived = refs[14:26], refs[26]
    copies = fetch(list(zip(sources, scratch)), arrived)
    u_ref, v_ref = scratch[:2]
    element_ref, local_ref, scale_ref, owner_ref, cell_ref = scratch[7:]
    f32 = jnp.float32
    own_ref[30:32] = jnp.zeros((2, 8, 128), f32)
    points_ref[...] = jnp.zeros((8, 128), f32)
    for copy in copies:
        copy.wait()
    for i in range(15):
        own_ref[i] = u_ref[i]
        own_ref[15 + i] = v_ref[i]
    for i, ref in enumerate(scratch[2:7]):
        both = ref[...].astype(f32)
        own_ref[30, i:i + 1, :] = jnp.broadcast_to(both[:, 0:1], (1, 128))
        own_ref[31, i:i + 1, :] = jnp.broadcast_to(both[:, 1:2], (1, 128))
    points_ref[0:2, 0:64] = local_ref[...]
    points_ref[2:3, 0:64] = (element_ref[1:2, :] % 2).astype(f32)
    points_ref[3:4, 0:64] = scale_ref[...]
    points_ref[4:5, 0:64] = owner_ref[...].astype(f32)
    points_ref[5:6, 0:64] = (cell_ref[...] + 1).astype(f32)


def pack(*arrays):
    f32 = jnp.float32
    hbm, vmem = pl.BlockSpec(memory_space=pltpu.HBM), pl.BlockSpec(memory_space=pltpu.VMEM)
    return pl.pallas_call(
        pack_kernel,
        in_specs=[hbm] * 12,
        out_specs=(vmem, vmem),
        scratch_shapes=[pltpu.VMEM(a.shape, a.dtype) for a in arrays] + [pltpu.SemaphoreType.DMA((12,))],
        out_shape=(
            jax.ShapeDtypeStruct((32, 8, 128), f32),
            jax.ShapeDtypeStruct((8, 128), f32),
        ),
        name="pack",
    )(*arrays)


def near_columns(target, first, source, upward):
    row = lax.broadcasted_iota(jnp.int32, (8, 128), 0)
    for i in range(15):
        u, v = source[i], source[15 + i]
        start = jnp.broadcast_to(v[0:1, :], (8, 128))
        target[first + i] = jnp.where((row == 5) & jnp.logical_not(upward), start, u)
    target[first + 15] = jnp.where(upward, source[31], source[30])


def chip_kernel(own_ref, sib_ref, out_ref):
    out_ref[0:32] = own_ref[...]
    near_columns(out_ref, 32, sib_ref, lax.axis_index("mer_2") == 1)


def forward_kernel(cross_ref, out_ref):
    near_columns(out_ref, 0, cross_ref, lax.axis_index("mer_2") == 0)


def chip_message(own, sib):
    return pl.pallas_call(
        chip_kernel, out_shape=jax.ShapeDtypeStruct((48, 8, 128), jnp.float32),
        compiler_params=GRANT, name="chip",
    )(own, sib)


def forward_message(cross):
    return pl.pallas_call(
        forward_kernel, out_shape=jax.ShapeDtypeStruct((16, 8, 128), jnp.float32),
        compiler_params=GRANT, name="forward",
    )(cross)


def step_kernel(own_ref, sib_ref, cross_ref, forward_ref, u_ref, gather_ref,
                ucol, vcol, coef, state, field):
    core, az = lax.axis_index("mer_2"), lax.axis_index("az")
    is_low = core == 0

    def left(i):
        return jnp.where(is_low, cross_ref[i], sib_ref[i])

    def right(i):
        return jnp.where(is_low, sib_ref[i], cross_ref[i])

    def far_left(i):
        return jnp.where(is_low, cross_ref[32 + i], forward_ref[i])

    def far_right(i):
        return jnp.where(is_low, forward_ref[i], cross_ref[32 + i])

    zero8 = jnp.zeros((8, 128), jnp.float32)
    for i in range(15):
        ucol[i, 0:8, :] = far_left(i)
        ucol[i, 8:16, :] = left(i)
        ucol[i, 16:24, :] = own_ref[i]
        ucol[i, 24:32, :] = right(i)
        high = far_right(i)
        ucol[i, 32:40, :] = high
        vcol[i, 0:8, :] = zero8
        vcol[i, 8:16, :] = left(15 + i)
        vcol[i, 16:24, :] = own_ref[15 + i]
        vcol[i, 24:32, :] = right(15 + i)
        vcol[i, 32:40, :] = zero8
        vcol[i, 32:33, :] = high[5:6, :]
    l0, l1, r0, r1 = left(30), left(31), right(30), right(31)
    sources = (far_left(15), l0, l1, own_ref[30], own_ref[31], r0, r1, far_right(15))
    for i in range(5):
        for e, tile in enumerate(sources):
            coef[i, e:e + 1, :] = tile[i:i + 1, :]

    lane = lax.broadcasted_iota(jnp.int32, (8, 128), 1)
    order = ((az * 128 + lane) // 2).astype(jnp.float32)
    ratio = order * (1.0 / ORDERS)
    mask = jnp.where(order < coef[4], 1.0, 0.0)
    is_even = lane % 2 == 0
    stiff = coef[0] * mask
    hoop = coef[1] * mask * ratio * ratio
    couple = coef[2] * mask * ratio
    couple_even = jnp.where(is_even, couple, 0.0)
    couple_odd = jnp.where(is_even, 0.0, -couple)
    density = coef[3]
    present = density > 0.0
    inner = jnp.where(present, step_scale / jnp.where(present, density, 1.0), 0.0)
    shared_density = density + pltpu.roll(density, 1, 0)
    edge = jnp.where(present, step_scale / jnp.where(present, shared_density, 1.0), 0.0)
    field[0], field[1], field[2], field[3], field[4], field[5] = (
        stiff, hoop, couple_even, couple_odd, inner, edge)

    for i in range(15):
        for b in range(5):
            u = ucol[i, pl.ds(4 + b, 8, stride=4), :]
            state[0, i, b] = u
            if b < 4:
                state[1, i, b] = u - vcol[i, pl.ds(4 + b, 8, stride=4), :]

    rows = stiffness_rows()

    def one_step(n, carry):
        now = lax.rem(n, 2)
        other = 1 - now
        stiff, hoop = field[0], field[1]
        couple_even, couple_odd = field[2], field[3]
        inner, edge = field[4], field[5]

        def coupled(x):
            return pltpu.roll(x, 127, 1) * couple_even + pltpu.roll(x, 1, 1) * couple_odd

        for s in range(3):
            u = [[state[now, 5 * s + a, b] for b in range(5)] for a in range(5)]
            for a in range(5):
                forces = []
                for b in range(5):
                    total = u[a][b] * float(rows[a, a] + rows[b, b])
                    for other_a in range(5):
                        if other_a != a:
                            total = total + u[other_a][b] * float(rows[a, other_a])
                    for other_b in range(5):
                        if other_b != b:
                            total = total + u[a][other_b] * float(rows[b, other_b])
                    force = -(stiff * total + hoop * u[a][b])
                    if s == 0:
                        force = force + coupled(state[now, 10 + a, b])
                    if s == 2:
                        force = force - coupled(state[now, a, b])
                    forces.append(force)
                forces[0] = forces[0] + pltpu.roll(forces[4], 1, 0)
                for b in range(4):
                    following = (
                        2.0 * u[a][b] - state[other, 5 * s + a, b]
                        + (edge if b == 0 else inner) * forces[b]
                    )
                    state[other, 5 * s + a, b] = following
                    if b == 0:
                        state[other, 5 * s + a, 4] = pltpu.roll(following, 7, 0)
        return carry

    lax.fori_loop(0, STEPS, one_step, 0)
    last = STEPS % 2
    for i in range(15):
        for b in range(4):
            ucol[i, pl.ds(4 + b, 8, stride=4), :] = state[last, i, b]
    for q in range(4):
        gather_ref[q, 15:17] = jnp.zeros((2, 8, 128), jnp.float32)
    for i in range(15):
        own = ucol[i, 16:24, :]
        rim = ucol[i, 24:25, :]
        u_ref[i] = own
        for q in range(4):
            gather_ref[q, i] = own
            gather_ref[q, 15 + i // 8, i % 8:i % 8 + 1, :] = rim


def march(own, sib, cross, forward):
    f32 = jnp.float32
    vmem = pl.BlockSpec(memory_space=pltpu.VMEM)
    return pl.pallas_call(
        step_kernel,
        in_specs=[vmem] * 4,
        out_specs=(vmem, vmem),
        out_shape=(
            jax.ShapeDtypeStruct((15, 8, 128), f32),
            jax.ShapeDtypeStruct((4, 17, 8, 128), f32),
        ),
        scratch_shapes=[
            pltpu.VMEM((15, 40, 128), f32),
            pltpu.VMEM((15, 40, 128), f32),
            pltpu.VMEM((5, 8, 128), f32),
            pltpu.VMEM((2, 15, 5, 8, 128), f32),
            pltpu.VMEM((6, 8, 128), f32),
        ],
        compiler_params=GRANT,
        name="march",
    )(own, sib, cross, forward)


def weight_kernel(points_ref, table_ref, weight_ref, point_ref, basis_ref):
    f32, bf16 = jnp.float32, jnp.bfloat16
    az = lax.axis_index("az")
    diagonal = (lax.broadcasted_iota(jnp.int32, (64, 128), 0)
                == lax.broadcasted_iota(jnp.int32, (64, 128), 1))

    def upright(line):
        return jnp.sum(jnp.where(diagonal, line, 0.0), axis=1, keepdims=True)

    xi, eta, second, scale, owner, code = (upright(points_ref[i:i + 1, :]) for i in range(6))

    def basis(x, rows):
        d1, d2, d3, d4 = x - rows[0], x - rows[1], x - rows[2], x - rows[3]
        d12, d34 = d1 * d2, d3 * d4
        return d12 * d34 * rows[4], ((d1 + d2) * d34 + d12 * (d3 + d4)) * rows[4]

    lanes = [table_ref[1024 + i:1025 + i, :] for i in range(16)]
    value_a, slope_a = basis(xi, lanes[0:5])
    first_b = basis(eta, lanes[5:10])
    second_b = basis(eta, lanes[10:15])
    value_b = jnp.where(second > 0.5, second_b[0], first_b[0])
    slope_b = jnp.where(second > 0.5, second_b[1], first_b[1])
    around = value_a * value_b * scale
    point = split(jnp.concatenate([slope_a * value_b, value_a * slope_b, around], axis=0))
    point_ref[0, 0:192] = point[0]
    point_ref[1, 0:192] = point[1]

    lane = lax.broadcasted_iota(jnp.int32, (64, 128), 1)
    sub = lax.broadcasted_iota(jnp.int32, (64, 128), 0)
    owners = points_ref[4:5, :]
    rank = jnp.sum(jnp.where((owner == owners) & (sub < lane), 1.0, 0.0), axis=0, keepdims=True)
    slot = owners * 2.0 + rank
    row = lax.broadcasted_iota(jnp.int32, (256, 128), 0)
    column = lax.broadcasted_iota(jnp.int32, (256, 128), 1)
    row_slot = (row % 64) * 4 + row // 64
    place = jnp.where((slot == row_slot.astype(f32)) & (column < 64), 1.0, 0.0).astype(bf16)[:, :64]
    for n in range(2):
        for d in range(3):
            weight_ref[2 * d + n] = dot(place, point[n][64 * d:64 * d + 64]).astype(bf16)

    upright_slot = upright(slot)
    group = (lane // 32).astype(f32)
    mine = upright_slot - 4.0 * jnp.floor(upright_slot * 0.25) == group
    point_ref[0, 192:256, 0:128] = jnp.where(mine & (lane % 32 == 31), code, 0.0).astype(bf16)
    point_ref[0, 192:256, 128:256] = jnp.where(mine & (lane % 32 < 18), 1.0, 0.0).astype(bf16)
    chip = jnp.where((jnp.floor(slot * 0.25) == sub.astype(f32)) & (lane < 64), 1.0, 0.0).astype(bf16)
    point_ref[1, 192:256, 0:128] = chip
    point_ref[1, 192:256, 128:256] = chip

    order = lax.broadcasted_iota(jnp.int32, (512, 128), 0) // 2
    turns = (order * az) % 4
    along = jnp.where(turns == 0, 1.0, jnp.where(turns == 2, -1.0, 0.0))
    across = jnp.where(turns == 1, 1.0, jnp.where(turns == 3, -1.0, 0.0))
    ratio = order.astype(f32) * (1.0 / ORDERS)
    first, other = slice(0, 512), slice(512, 1024)
    low_lanes, edge_lanes = slice(0, 128), slice(128, 256)
    value = along * table_ref[first, low_lanes] + across * table_ref[other, low_lanes]
    slope = ratio * (along * table_ref[other, low_lanes] - across * table_ref[first, low_lanes])
    edge_value = along * table_ref[first, edge_lanes] + across * table_ref[other, edge_lanes]
    edge_slope = ratio * (along * table_ref[other, edge_lanes] - across * table_ref[first, edge_lanes])
    kind = ((lax.broadcasted_iota(jnp.int32, (512, 128), 1) % 32) % 9) % 3
    edge = jnp.where(kind == 2, edge_slope, edge_value)
    for i, block in enumerate((value, slope, edge)):
        high, low = split(block)
        basis_ref[0, :, 128 * i:128 * i + 128] = high
        basis_ref[1, :, 128 * i:128 * i + 128] = low


def point_weights(points):
    bf16 = jnp.bfloat16
    return pl.pallas_call(
        weight_kernel,
        out_shape=(
            jax.ShapeDtypeStruct((6, 256, 256), bf16),
            jax.ShapeDtypeStruct((2, 256, 256), bf16),
            jax.ShapeDtypeStruct((2, 512, 384), bf16),
        ),
        compiler_params=GRANT,
        name="weights",
    )(points, jnp.asarray(constant_table()))


def thrice(a, b):
    return dot(a[0], b[0]) + (dot(a[1], b[0]) + dot(a[0], b[1]))


def message_kernel(nodes_ref, weight_ref, point_ref, basis_ref, out_ref):
    f32 = jnp.float32
    coefs = jnp.concatenate([nodes_ref[q].reshape(136, 128) for q in range(4)], axis=1)
    samples = thrice(split(coefs), (basis_ref[0], basis_ref[1]))
    row = lax.broadcasted_iota(jnp.int32, (136, 128), 0)
    component = jnp.where(row < 120, row // 40, (row - 120) // 5)
    pad = jnp.zeros((120, 384), f32)
    values, slopes, edges = samples[:, :128], samples[:, 128:256], samples[:, 256:]

    def spread(block):
        parts = jnp.concatenate([jnp.where(component == s, block, 0.0) for s in range(3)], axis=1)
        return split(jnp.concatenate([parts, pad], axis=0))

    by_kind = (spread(values), None, spread(slopes))
    for d in range(3):
        field = by_kind[0] if d < 2 else by_kind[2]
        rows = thrice((weight_ref[2 * d], weight_ref[2 * d + 1]), field)
        for s in range(3):
            for c in range(4):
                out_ref[pl.ds(4 * (3 * s + d) + c, 64, stride=ROWS), :] = (
                    rows[64 * c:64 * c + 64, 128 * s:128 * s + 128])

    lane = lax.broadcasted_iota(jnp.int32, (136, 128), 1)
    edges = jnp.where(((lane % 32) % 9) // 3 == component, edges, 0.0)
    edges = split(jnp.concatenate([edges, pad[:, :128]], axis=0))
    rows = thrice((point_ref[0, 0:192], point_ref[1, 0:192]), edges)
    lane = lax.broadcasted_iota(jnp.int32, (64, 128), 1)
    kind = ((lane % 32) % 9) % 3
    extra = jnp.where(kind == 0, rows[:64], jnp.where(kind == 1, rows[64:128], rows[128:]))
    extra = (extra * point_ref[0, 192:256, 128:256].astype(f32)
             + point_ref[0, 192:256, 0:128].astype(f32))
    chip = point_ref[1, 192:256, 0:64]
    high, low = split(extra)
    out_ref[pl.ds(36, 64, stride=ROWS), :] = dot(chip, high) + dot(chip, low)


def messages(nodes, *weights):
    return pl.pallas_call(
        message_kernel,
        out_shape=jax.ShapeDtypeStruct((64 * ROWS, 128), jnp.float32),
        compiler_params=GRANT,
        name="messages",
    )(nodes, *weights)


def rims_kernel(own_ref, sib_ref, first_ref, last_ref):
    lane = lax.broadcasted_iota(jnp.int32, (32, 128), 1)
    for n, ref in enumerate((own_ref, sib_ref)):
        first = jnp.zeros((32, 128), jnp.float32)
        last = jnp.zeros((32, 128), jnp.float32)
        for g in range(9):
            first = jnp.where(lane == 9 + g, ref[g, :, 0:1], first)
            last = jnp.where(lane == g, ref[g, :, 127:128], last)
        first_ref[n] = first
        last_ref[n] = last


def rims(own, sib):
    shape = jax.ShapeDtypeStruct((2, 32, 128), jnp.float32)
    return pl.pallas_call(
        rims_kernel, out_shape=(shape, shape), compiler_params=GRANT, name="rims",
    )(own, sib)


def voxel_kernel(arrived_ref, own_ref, sib_ref, before_ref, after_ref, out_ref):
    is_low = lax.axis_index("mer_2") == 0
    f32 = jnp.float32
    tail = arrived_ref[pl.ds(36, 64, stride=ROWS), :]
    lane = lax.broadcasted_iota(jnp.int32, (64, 128), 1)
    wanted = (lane % 32 + 1).astype(f32)
    sorting = jnp.concatenate(
        [
            jnp.where((lane // 32 == c // 2) & (tail[:, 32 * c + 31:32 * c + 32] == wanted), 1.0, 0.0)
            for c in range(4)
        ],
        axis=0,
    ).astype(jnp.bfloat16)

    def sorted_sum(rows):
        high, low = split(rows)
        both = lax.dot_general(
            sorting, jnp.concatenate([high, low], axis=1), (((0,), (0,)), ((), ())),
            preferred_element_type=f32,
        )
        return both[:64, :128] + both[:64, 128:]

    totals = [jnp.zeros((32, 128), f32) for _ in range(2)]
    for g in range(9):
        summed = sorted_sum(jnp.concatenate(
            [arrived_ref[pl.ds(4 * g + c, 64, stride=ROWS), :] for c in range(4)], axis=0))
        mine, theirs = own_ref[g], sib_ref[g]
        totals[0] = totals[0] + summed[:32] * jnp.where(is_low, mine, theirs)
        totals[1] = totals[1] + summed[32:] * jnp.where(is_low, theirs, mine)
    shifted = [tail] + [pltpu.roll(tail, 128 - 32 * c, 1) for c in range(1, 4)]
    ends = sorted_sum(jnp.concatenate([jnp.where(lane < 18, x, 0.0) for x in shifted], axis=0))
    own_edge, sib_edge = before_ref[0] + after_ref[0], before_ref[1] + after_ref[1]
    side = (ends[:32] * jnp.where(is_low, own_edge, sib_edge), ends[32:] * jnp.where(is_low, sib_edge, own_edge))
    out_ref[0] = totals[0]
    out_ref[1] = totals[1]
    for core in range(2):
        product = side[core]
        small = lax.broadcasted_iota(jnp.int32, (32, 128), 1)
        west = jnp.sum(jnp.where(small < 9, product, 0.0), axis=1, keepdims=True)
        east = jnp.sum(jnp.where((small >= 9) & (small < 18), product, 0.0), axis=1, keepdims=True)
        out_ref[2 + core] = jnp.where(small == 127, west, jnp.where(small == 0, east, 0.0))


def voxels(arrived, own, sib, before, after):
    f32 = jnp.float32
    return pl.pallas_call(
        voxel_kernel,
        out_shape=jax.ShapeDtypeStruct((4, 32, 128), f32),
        compiler_params=GRANT,
        name="voxels",
    )(arrived, own, sib, before, after)


def total_kernel(mine_ref, theirs_ref, base_ref, edge_ref, full, framed):
    is_low = lax.axis_index("mer_2") == 0
    low = mine_ref[0] + theirs_ref[0]
    high = mine_ref[1] + theirs_ref[1]
    raw = jnp.where(is_low, low, high)
    ends = jnp.where(is_low, mine_ref[2] + theirs_ref[2], mine_ref[3] + theirs_ref[3])
    full[0] = low
    full[1] = high
    low_first, low_last = full[0, pl.ds(0, 8, stride=4), :], full[0, pl.ds(3, 8, stride=4), :]
    high_first, high_last = full[1, pl.ds(0, 8, stride=4), :], full[1, pl.ds(3, 8, stride=4), :]
    edge_ref[...] = jnp.where(is_low, low_first, high_last)
    framed[0:8] = jnp.zeros((8, 128), jnp.float32)
    framed[8:40] = raw
    framed[40:48] = jnp.zeros((8, 128), jnp.float32)
    lane = lax.broadcasted_iota(jnp.int32, (32, 128), 1)
    row = lax.broadcasted_iota(jnp.int32, (32, 128), 0)
    west = pltpu.roll(jnp.where(lane == 127, ends, raw), 1, 1)
    east = pltpu.roll(jnp.where(lane == 0, ends, raw), 127, 1)
    neighbours = framed[4:36] + framed[12:44] + west + east
    down = jnp.where(row % 4 == 0, 0.0, framed[7:39])
    up = jnp.where(row % 4 == 3, 0.0, framed[9:41])
    neighbours = neighbours + down + up
    base_ref[...] = raw + smooth_rate * (neighbours - 6.0 * raw)
    base_ref[pl.ds(0, 8, stride=4), :] += jnp.where(is_low, 0.0, smooth_rate * low_last)
    base_ref[pl.ds(3, 8, stride=4), :] += jnp.where(is_low, smooth_rate * high_first, 0.0)


def total(mine, theirs):
    f32 = jnp.float32
    return pl.pallas_call(
        total_kernel,
        out_shape=(jax.ShapeDtypeStruct((32, 128), f32), jax.ShapeDtypeStruct((8, 128), f32)),
        scratch_shapes=[pltpu.VMEM((2, 32, 128), f32), pltpu.VMEM((48, 128), f32)],
        compiler_params=GRANT,
        name="total",
    )(mine, theirs)


def smooth_kernel(base_ref, outer_ref, out_ref):
    is_low = lax.axis_index("mer_2") == 0
    outer = smooth_rate * outer_ref[...]
    out_ref[...] = base_ref[...]
    out_ref[pl.ds(0, 8, stride=4), :] += jnp.where(is_low, outer, 0.0)
    out_ref[pl.ds(3, 8, stride=4), :] += jnp.where(is_low, 0.0, outer)


def smooth(base, outer):
    return pl.pallas_call(
        smooth_kernel,
        out_shape=jax.ShapeDtypeStruct((32, 128), jnp.float32),
        compiler_params=GRANT,
        name="smooth",
    )(base, outer)


def on_device(
    displacement,
    velocity,
    modulus,
    hoop_strength,
    coupling,
    density,
    order_count,
    point_element,
    point_local,
    azimuth_scale,
    point_owner,
    point_cell,
    adjoint_strain,
):
    count = lax.axis_size(MER)
    az_count = lax.axis_size("az")
    swap = [(0, 1), (1, 0)]
    cross = [(c, c + 1) for c in range(1, count - 1, 2)] + [(c + 1, c) for c in range(1, count - 1, 2)]
    ahead = [(i, (i + 1) % az_count) for i in range(az_count)]

    own, points = pack(
        displacement.reshape(15, 8, 128), velocity.reshape(15, 8, 128),
        modulus, hoop_strength, coupling, density, order_count,
        point_element.T, point_local.T, azimuth_scale.reshape(1, 64), point_owner.reshape(1, 64),
        point_cell.reshape(1, 64),
    )
    sib = lax.ppermute(own, "mer_2", swap)
    outer = lax.ppermute(chip_message(own, sib), MER, cross)
    forward = lax.ppermute(forward_message(outer), "mer_2", swap)
    final, spread = march(own, sib, outer, forward)

    weights = point_weights(points)
    nodes = lax.all_to_all(spread, "az", 0, 0, tiled=True)
    outgoing = messages(nodes, *weights)
    arrived = lax.all_to_all(outgoing.reshape(64, ROWS, 1, 128), SIDES, 0, 0, tiled=True)
    arrived = arrived.reshape(64 * ROWS, 128)

    adjoint = adjoint_strain.reshape(9, 32, 128)
    adjoint_sib = lax.ppermute(adjoint, "mer_2", swap)
    first, last = rims(adjoint, adjoint_sib)
    before = lax.ppermute(last, "az", ahead)
    after = lax.ppermute(first, "az", [(b, a) for a, b in ahead])
    part = voxels(arrived, adjoint, adjoint_sib, before, after)
    base, edge = total(part, lax.ppermute(part, "mer_2", swap))
    kernel = smooth(base, lax.ppermute(edge, MER, cross))
    return final.reshape(3, 5, 8, 128), kernel.reshape(8, 4, 128)


def solution(mesh):
    torus = Mesh(mesh.devices.reshape(8, 8, 2, mesh.shape["az"]), ("mer_0", "mer_1", "mer_2", "az"))
    return jax.shard_map(
        on_device,
        mesh=torus,
        in_specs=(
            P(None, None, MER, "az"),
            P(None, None, MER, "az"),
            P(None, MER),
            P(None, MER),
            P(None, MER),
            P(None, MER),
            P(None, MER),
            P(MER, None),
            P(MER, None),
            P(MER),
            P(MER, None),
            P(MER),
            P(None, None, MER, "az"),
        ),
        out_specs=(P(None, None, MER, "az"), P(None, MER, "az")),
        check_vma=False,
    )
```

```python
import math

import jax
import jax.numpy as jnp
import numpy as np
from jax import lax
from jax.experimental import pallas as pl
from jax.experimental.pallas import tpu as pltpu
from jax.sharding import Mesh
from jax.sharding import PartitionSpec as P

ORDERS = 256
STEPS = 3
MER = ("mer_0", "mer_1", "mer_2")
SIDES = ("mer_0", "mer_1")

GRANT = pltpu.CompilerParams(vmem_limit_bytes=16 << 20)

step_scale = 0.015
smooth_rate = 0.125


def gll_tables():
    nodes = np.array([-1.0, -math.sqrt(3.0 / 7.0), 0.0, math.sqrt(3.0 / 7.0), 1.0])
    weights = np.array([0.1, 49.0 / 90.0, 32.0 / 45.0, 49.0 / 90.0, 0.1])
    derivative = np.zeros((5, 5))
    for i in range(5):
        for j in range(5):
            if i == j:
                derivative[i, j] = sum(1.0 / (nodes[i] - nodes[l]) for l in range(5) if l != i)
            else:
                scale_i = np.prod([nodes[i] - nodes[l] for l in range(5) if l != i])
                scale_j = np.prod([nodes[j] - nodes[l] for l in range(5) if l != j])
                derivative[i, j] = scale_i / (scale_j * (nodes[i] - nodes[j]))
    return nodes, weights, derivative


def stiffness_rows():
    _, weights, derivative = gll_tables()
    return (derivative.T @ np.diag(weights) @ derivative) / weights[:, None]


ROWS = 37


def basis_tables():
    k = np.arange(2 * ORDERS)
    order = k // 2
    j = np.zeros(256, np.int64)
    j[:128] = np.arange(128)
    edge = np.arange(128) % 32
    j[128:] = np.where(edge < 9, -1, np.where(edge < 18, 128, 0))
    angle = (order[:, None] * j[None, :] % (2 * ORDERS)) * (2.0 * math.pi / (2 * ORDERS))
    even = (k % 2 == 0)[:, None]
    value = np.where(even, np.cos(angle), np.sin(angle))
    slope = np.where(even, -np.sin(angle), np.cos(angle))
    return (np.stack([value, slope]) / math.sqrt(ORDERS)).astype(np.float32)


def lane_tables():
    nodes = gll_tables()[0]
    rows = np.zeros((16, 256), np.float32)
    for r in range(135):
        if r < 120:
            s, a, c = r // 40, r // 8 % 5, r % 8
        else:
            s, a, c = (r - 120) // 5, (r - 120) % 5, 8

        def place(first, n):
            others = [l for l in range(5) if l != n]
            for i, l in enumerate(others):
                rows[first + i, r] = nodes[l]
            rows[first + 4, r] = 1.0 / np.prod([nodes[n] - nodes[l] for l in others])

        place(0, a)
        if c <= 4:
            place(5, c)
        if c >= 4:
            place(10, c - 4)
        rows[15, r] = s + 1
    return rows


def constant_table():
    return np.concatenate([basis_tables().reshape(1024, 256), lane_tables()], axis=0)


def split(x):
    high = x.astype(jnp.bfloat16)
    low = (x - high.astype(jnp.float32)).astype(jnp.bfloat16)
    return high, low


def dot(a, b):
    return jnp.dot(a, b, preferred_element_type=jnp.float32)


def fetch(pairs, arrived):
    copies = [pltpu.make_async_copy(a, b, arrived.at[i]) for i, (a, b) in enumerate(pairs)]
    for copy in copies:
        copy.start()
    return copies


def pack_kernel(*refs):
    sources, (own_ref, near_ref, points_ref) = refs[:12], refs[12:15]
    scratch, arrived = refs[15:27], refs[27]
    copies = fetch(list(zip(sources, scratch)), arrived)
    u_ref, v_ref = scratch[:2]
    element_ref, local_ref, scale_ref, owner_ref, cell_ref = scratch[7:]
    f32 = jnp.float32
    own_ref[30:32] = jnp.zeros((2, 8, 128), f32)
    points_ref[...] = jnp.zeros((8, 128), f32)
    for copy in copies:
        copy.wait()
    for i in range(15):
        own_ref[i] = u_ref[i]
        own_ref[15 + i] = v_ref[i]
    for i, ref in enumerate(scratch[2:7]):
        both = ref[...].astype(f32)
        own_ref[30, i:i + 1, :] = jnp.broadcast_to(both[:, 0:1], (1, 128))
        own_ref[31, i:i + 1, :] = jnp.broadcast_to(both[:, 1:2], (1, 128))
    near_columns(near_ref, own_ref, lax.axis_index("mer_2") == 1)
    points_ref[0:2, 0:64] = local_ref[...]
    points_ref[2:3, 0:64] = (element_ref[1:2, :] % 2).astype(f32)
    points_ref[3:4, 0:64] = scale_ref[...]
    points_ref[4:5, 0:64] = owner_ref[...].astype(f32)
    points_ref[5:6, 0:64] = (cell_ref[...] + 1).astype(f32)


def pack(*arrays):
    f32 = jnp.float32
    hbm, vmem = pl.BlockSpec(memory_space=pltpu.HBM), pl.BlockSpec(memory_space=pltpu.VMEM)
    return pl.pallas_call(
        pack_kernel,
        in_specs=[hbm] * 12,
        out_specs=(vmem, vmem, vmem),
        scratch_shapes=[pltpu.VMEM(a.shape, a.dtype) for a in arrays] + [pltpu.SemaphoreType.DMA((12,))],
        out_shape=(
            jax.ShapeDtypeStruct((32, 8, 128), f32),
            jax.ShapeDtypeStruct((16, 8, 128), f32),
            jax.ShapeDtypeStruct((8, 128), f32),
        ),
        name="pack",
    )(*arrays)


def near_columns(target, source, upward):
    row = lax.broadcasted_iota(jnp.int32, (8, 128), 0)
    for i in range(15):
        u, v = source[i], source[15 + i]
        start = jnp.broadcast_to(v[0:1, :], (8, 128))
        target[i] = jnp.where((row == 5) & jnp.logical_not(upward), start, u)
    target[15] = jnp.where(upward, source[31], source[30])


def chip_kernel(own_ref, sib_ref, out_ref):
    out_ref[0:32] = own_ref[...]
    near_columns(out_ref.at[32:48], sib_ref, lax.axis_index("mer_2") == 1)


def chip_message(own, sib):
    return pl.pallas_call(
        chip_kernel, out_shape=jax.ShapeDtypeStruct((48, 8, 128), jnp.float32),
        compiler_params=GRANT, name="chip",
    )(own, sib)


def step_kernel(own_ref, sib_ref, cross_ref, diagonal_ref, u_ref, gather_ref,
                ucol, vcol, coef, state, field):
    core, az = lax.axis_index("mer_2"), lax.axis_index("az")
    is_low = core == 0

    def left(i):
        return jnp.where(is_low, cross_ref[i], sib_ref[i])

    def right(i):
        return jnp.where(is_low, sib_ref[i], cross_ref[i])

    def far_left(i):
        return jnp.where(is_low, cross_ref[32 + i], diagonal_ref[i])

    def far_right(i):
        return jnp.where(is_low, diagonal_ref[i], cross_ref[32 + i])

    zero8 = jnp.zeros((8, 128), jnp.float32)
    for i in range(15):
        ucol[i, 0:8, :] = far_left(i)
        ucol[i, 8:16, :] = left(i)
        ucol[i, 16:24, :] = own_ref[i]
        ucol[i, 24:32, :] = right(i)
        high = far_right(i)
        ucol[i, 32:40, :] = high
        vcol[i, 0:8, :] = zero8
        vcol[i, 8:16, :] = left(15 + i)
        vcol[i, 16:24, :] = own_ref[15 + i]
        vcol[i, 24:32, :] = right(15 + i)
        vcol[i, 32:40, :] = zero8
        vcol[i, 32:33, :] = high[5:6, :]
    l0, l1, r0, r1 = left(30), left(31), right(30), right(31)
    sources = (far_left(15), l0, l1, own_ref[30], own_ref[31], r0, r1, far_right(15))
    for i in range(5):
        for e, tile in enumerate(sources):
            coef[i, e:e + 1, :] = tile[i:i + 1, :]

    lane = lax.broadcasted_iota(jnp.int32, (8, 128), 1)
    order = ((az * 128 + lane) // 2).astype(jnp.float32)
    ratio = order * (1.0 / ORDERS)
    mask = jnp.where(order < coef[4], 1.0, 0.0)
    is_even = lane % 2 == 0
    stiff = coef[0] * mask
    hoop = coef[1] * mask * ratio * ratio
    couple = coef[2] * mask * ratio
    couple_even = jnp.where(is_even, couple, 0.0)
    couple_odd = jnp.where(is_even, 0.0, -couple)
    density = coef[3]
    present = density > 0.0
    inner = jnp.where(present, step_scale / jnp.where(present, density, 1.0), 0.0)
    shared_density = density + pltpu.roll(density, 1, 0)
    edge = jnp.where(present, step_scale / jnp.where(present, shared_density, 1.0), 0.0)
    field[0], field[1], field[2], field[3], field[4], field[5] = (
        stiff, hoop, couple_even, couple_odd, inner, edge)

    for i in range(15):
        for b in range(5):
            u = ucol[i, pl.ds(4 + b, 8, stride=4), :]
            state[0, i, b] = u
            if b < 4:
                state[1, i, b] = u - vcol[i, pl.ds(4 + b, 8, stride=4), :]

    rows = stiffness_rows()

    def one_step(n, carry):
        now = lax.rem(n, 2)
        other = 1 - now
        stiff, hoop = field[0], field[1]
        couple_even, couple_odd = field[2], field[3]
        inner, edge = field[4], field[5]

        def coupled(x):
            return pltpu.roll(x, 127, 1) * couple_even + pltpu.roll(x, 1, 1) * couple_odd

        for s in range(3):
            u = [[state[now, 5 * s + a, b] for b in range(5)] for a in range(5)]
            for a in range(5):
                forces = []
                for b in range(5):
                    total = u[a][b] * float(rows[a, a] + rows[b, b])
                    for other_a in range(5):
                        if other_a != a:
                            total = total + u[other_a][b] * float(rows[a, other_a])
                    for other_b in range(5):
                        if other_b != b:
                            total = total + u[a][other_b] * float(rows[b, other_b])
                    force = -(stiff * total + hoop * u[a][b])
                    if s == 0:
                        force = force + coupled(state[now, 10 + a, b])
                    if s == 2:
                        force = force - coupled(state[now, a, b])
                    forces.append(force)
                forces[0] = forces[0] + pltpu.roll(forces[4], 1, 0)
                for b in range(4):
                    following = (
                        2.0 * u[a][b] - state[other, 5 * s + a, b]
                        + (edge if b == 0 else inner) * forces[b]
                    )
                    state[other, 5 * s + a, b] = following
                    if b == 0:
                        state[other, 5 * s + a, 4] = pltpu.roll(following, 7, 0)
        return carry

    lax.fori_loop(0, STEPS, one_step, 0)
    last = STEPS % 2
    for i in range(15):
        for b in range(4):
            ucol[i, pl.ds(4 + b, 8, stride=4), :] = state[last, i, b]
    for q in range(4):
        gather_ref[q, 15:17] = jnp.zeros((2, 8, 128), jnp.float32)
    for i in range(15):
        own = ucol[i, 16:24, :]
        rim = ucol[i, 24:25, :]
        u_ref[i] = own
        for q in range(4):
            gather_ref[q, i] = own
            gather_ref[q, 15 + i // 8, i % 8:i % 8 + 1, :] = rim


def march(own, sib, cross, diagonal):
    f32 = jnp.float32
    vmem = pl.BlockSpec(memory_space=pltpu.VMEM)
    return pl.pallas_call(
        step_kernel,
        in_specs=[vmem] * 4,
        out_specs=(vmem, vmem),
        out_shape=(
            jax.ShapeDtypeStruct((15, 8, 128), f32),
            jax.ShapeDtypeStruct((4, 17, 8, 128), f32),
        ),
        scratch_shapes=[
            pltpu.VMEM((15, 40, 128), f32),
            pltpu.VMEM((15, 40, 128), f32),
            pltpu.VMEM((5, 8, 128), f32),
            pltpu.VMEM((2, 15, 5, 8, 128), f32),
            pltpu.VMEM((6, 8, 128), f32),
        ],
        compiler_params=GRANT,
        name="march",
    )(own, sib, cross, diagonal)


def weight_kernel(points_ref, table_ref, weight_ref, point_ref, basis_ref):
    f32, bf16 = jnp.float32, jnp.bfloat16
    az = lax.axis_index("az")
    diagonal = (lax.broadcasted_iota(jnp.int32, (64, 128), 0)
                == lax.broadcasted_iota(jnp.int32, (64, 128), 1))

    def upright(line):
        return jnp.sum(jnp.where(diagonal, line, 0.0), axis=1, keepdims=True)

    xi, eta, second, scale, owner, code = (upright(points_ref[i:i + 1, :]) for i in range(6))

    def basis(x, rows):
        d1, d2, d3, d4 = x - rows[0], x - rows[1], x - rows[2], x - rows[3]
        d12, d34 = d1 * d2, d3 * d4
        return d12 * d34 * rows[4], ((d1 + d2) * d34 + d12 * (d3 + d4)) * rows[4]

    lanes = [table_ref[1024 + i:1025 + i, :] for i in range(16)]
    value_a, slope_a = basis(xi, lanes[0:5])
    first_b = basis(eta, lanes[5:10])
    second_b = basis(eta, lanes[10:15])
    value_b = jnp.where(second > 0.5, second_b[0], first_b[0])
    slope_b = jnp.where(second > 0.5, second_b[1], first_b[1])
    around = value_a * value_b * scale
    point = split(jnp.concatenate([slope_a * value_b, value_a * slope_b, around], axis=0))
    point_ref[0, 0:192] = point[0]
    point_ref[1, 0:192] = point[1]

    lane = lax.broadcasted_iota(jnp.int32, (64, 128), 1)
    sub = lax.broadcasted_iota(jnp.int32, (64, 128), 0)
    owners = points_ref[4:5, :]
    rank = jnp.sum(jnp.where((owner == owners) & (sub < lane), 1.0, 0.0), axis=0, keepdims=True)
    slot = owners * 2.0 + rank
    row = lax.broadcasted_iota(jnp.int32, (256, 128), 0)
    column = lax.broadcasted_iota(jnp.int32, (256, 128), 1)
    row_slot = (row % 64) * 4 + row // 64
    place = jnp.where((slot == row_slot.astype(f32)) & (column < 64), 1.0, 0.0).astype(bf16)[:, :64]
    for n in range(2):
        for d in range(3):
            weight_ref[2 * d + n] = dot(place, point[n][64 * d:64 * d + 64]).astype(bf16)

    upright_slot = upright(slot)
    group = (lane // 32).astype(f32)
    mine = upright_slot - 4.0 * jnp.floor(upright_slot * 0.25) == group
    point_ref[0, 192:256, 0:128] = jnp.where(mine & (lane % 32 == 31), code, 0.0).astype(bf16)
    point_ref[0, 192:256, 128:256] = jnp.where(mine & (lane % 32 < 18), 1.0, 0.0).astype(bf16)
    chip = jnp.where((jnp.floor(slot * 0.25) == sub.astype(f32)) & (lane < 64), 1.0, 0.0).astype(bf16)
    point_ref[1, 192:256, 0:128] = chip
    point_ref[1, 192:256, 128:256] = chip

    order = lax.broadcasted_iota(jnp.int32, (512, 128), 0) // 2
    turns = (order * az) % 4
    along = jnp.where(turns == 0, 1.0, jnp.where(turns == 2, -1.0, 0.0))
    across = jnp.where(turns == 1, 1.0, jnp.where(turns == 3, -1.0, 0.0))
    ratio = order.astype(f32) * (1.0 / ORDERS)
    first, other = slice(0, 512), slice(512, 1024)
    low_lanes, edge_lanes = slice(0, 128), slice(128, 256)
    value = along * table_ref[first, low_lanes] + across * table_ref[other, low_lanes]
    slope = ratio * (along * table_ref[other, low_lanes] - across * table_ref[first, low_lanes])
    edge_value = along * table_ref[first, edge_lanes] + across * table_ref[other, edge_lanes]
    edge_slope = ratio * (along * table_ref[other, edge_lanes] - across * table_ref[first, edge_lanes])
    kind = ((lax.broadcasted_iota(jnp.int32, (512, 128), 1) % 32) % 9) % 3
    edge = jnp.where(kind == 2, edge_slope, edge_value)
    for i, block in enumerate((value, slope, edge)):
        high, low = split(block)
        basis_ref[0, :, 128 * i:128 * i + 128] = high
        basis_ref[1, :, 128 * i:128 * i + 128] = low


def point_weights(points):
    bf16 = jnp.bfloat16
    return pl.pallas_call(
        weight_kernel,
        out_shape=(
            jax.ShapeDtypeStruct((6, 256, 256), bf16),
            jax.ShapeDtypeStruct((2, 256, 256), bf16),
            jax.ShapeDtypeStruct((2, 512, 384), bf16),
        ),
        compiler_params=GRANT,
        name="weights",
    )(points, jnp.asarray(constant_table()))


def thrice(a, b):
    return dot(a[0], b[0]) + (dot(a[1], b[0]) + dot(a[0], b[1]))


def message_kernel(nodes_ref, weight_ref, point_ref, basis_ref, out_ref):
    f32 = jnp.float32
    coefs = jnp.concatenate([nodes_ref[q].reshape(136, 128) for q in range(4)], axis=1)
    samples = thrice(split(coefs), (basis_ref[0], basis_ref[1]))
    row = lax.broadcasted_iota(jnp.int32, (136, 128), 0)
    component = jnp.where(row < 120, row // 40, (row - 120) // 5)
    pad = jnp.zeros((120, 384), f32)
    values, slopes, edges = samples[:, :128], samples[:, 128:256], samples[:, 256:]

    def spread(block):
        parts = jnp.concatenate([jnp.where(component == s, block, 0.0) for s in range(3)], axis=1)
        return split(jnp.concatenate([parts, pad], axis=0))

    by_kind = (spread(values), None, spread(slopes))
    for d in range(3):
        field = by_kind[0] if d < 2 else by_kind[2]
        rows = thrice((weight_ref[2 * d], weight_ref[2 * d + 1]), field)
        for s in range(3):
            for c in range(4):
                out_ref[pl.ds(4 * (3 * s + d) + c, 64, stride=ROWS), :] = (
                    rows[64 * c:64 * c + 64, 128 * s:128 * s + 128])

    lane = lax.broadcasted_iota(jnp.int32, (136, 128), 1)
    edges = jnp.where(((lane % 32) % 9) // 3 == component, edges, 0.0)
    edges = split(jnp.concatenate([edges, pad[:, :128]], axis=0))
    rows = thrice((point_ref[0, 0:192], point_ref[1, 0:192]), edges)
    lane = lax.broadcasted_iota(jnp.int32, (64, 128), 1)
    kind = ((lane % 32) % 9) % 3
    extra = jnp.where(kind == 0, rows[:64], jnp.where(kind == 1, rows[64:128], rows[128:]))
    extra = (extra * point_ref[0, 192:256, 128:256].astype(f32)
             + point_ref[0, 192:256, 0:128].astype(f32))
    chip = point_ref[1, 192:256, 0:64]
    high, low = split(extra)
    out_ref[pl.ds(36, 64, stride=ROWS), :] = dot(chip, high) + dot(chip, low)


def messages(nodes, *weights):
    return pl.pallas_call(
        message_kernel,
        out_shape=jax.ShapeDtypeStruct((64 * ROWS, 128), jnp.float32),
        compiler_params=GRANT,
        name="messages",
    )(nodes, *weights)


def rims_kernel(own_ref, sib_ref, first_ref, last_ref):
    lane = lax.broadcasted_iota(jnp.int32, (32, 128), 1)
    for n, ref in enumerate((own_ref, sib_ref)):
        first = jnp.zeros((32, 128), jnp.float32)
        last = jnp.zeros((32, 128), jnp.float32)
        for g in range(9):
            first = jnp.where(lane == 9 + g, ref[g, :, 0:1], first)
            last = jnp.where(lane == g, ref[g, :, 127:128], last)
        first_ref[n] = first
        last_ref[n] = last


def rims(own, sib):
    shape = jax.ShapeDtypeStruct((2, 32, 128), jnp.float32)
    return pl.pallas_call(
        rims_kernel, out_shape=(shape, shape), compiler_params=GRANT, name="rims",
    )(own, sib)


def voxel_kernel(arrived_ref, own_ref, sib_ref, before_ref, after_ref, out_ref):
    is_low = lax.axis_index("mer_2") == 0
    f32 = jnp.float32
    tail = arrived_ref[pl.ds(36, 64, stride=ROWS), :]
    lane = lax.broadcasted_iota(jnp.int32, (64, 128), 1)
    wanted = (lane % 32 + 1).astype(f32)
    sorting = jnp.concatenate(
        [
            jnp.where((lane // 32 == c // 2) & (tail[:, 32 * c + 31:32 * c + 32] == wanted), 1.0, 0.0)
            for c in range(4)
        ],
        axis=0,
    ).astype(jnp.bfloat16)

    def sorted_sum(rows):
        high, low = split(rows)
        both = lax.dot_general(
            sorting, jnp.concatenate([high, low], axis=1), (((0,), (0,)), ((), ())),
            preferred_element_type=f32,
        )
        return both[:64, :128] + both[:64, 128:]

    totals = [jnp.zeros((32, 128), f32) for _ in range(2)]
    for g in range(9):
        summed = sorted_sum(jnp.concatenate(
            [arrived_ref[pl.ds(4 * g + c, 64, stride=ROWS), :] for c in range(4)], axis=0))
        mine, theirs = own_ref[g], sib_ref[g]
        totals[0] = totals[0] + summed[:32] * jnp.where(is_low, mine, theirs)
        totals[1] = totals[1] + summed[32:] * jnp.where(is_low, theirs, mine)
    shifted = [tail] + [pltpu.roll(tail, 128 - 32 * c, 1) for c in range(1, 4)]
    ends = sorted_sum(jnp.concatenate([jnp.where(lane < 18, x, 0.0) for x in shifted], axis=0))
    own_edge, sib_edge = before_ref[0] + after_ref[0], before_ref[1] + after_ref[1]
    side = (ends[:32] * jnp.where(is_low, own_edge, sib_edge), ends[32:] * jnp.where(is_low, sib_edge, own_edge))
    out_ref[0] = totals[0]
    out_ref[1] = totals[1]
    for core in range(2):
        product = side[core]
        small = lax.broadcasted_iota(jnp.int32, (32, 128), 1)
        west = jnp.sum(jnp.where(small < 9, product, 0.0), axis=1, keepdims=True)
        east = jnp.sum(jnp.where((small >= 9) & (small < 18), product, 0.0), axis=1, keepdims=True)
        out_ref[2 + core] = jnp.where(small == 127, west, jnp.where(small == 0, east, 0.0))


def voxels(arrived, own, sib, before, after):
    f32 = jnp.float32
    return pl.pallas_call(
        voxel_kernel,
        out_shape=jax.ShapeDtypeStruct((4, 32, 128), f32),
        compiler_params=GRANT,
        name="voxels",
    )(arrived, own, sib, before, after)


def total_kernel(mine_ref, theirs_ref, base_ref, edge_ref, full, framed):
    is_low = lax.axis_index("mer_2") == 0
    low = mine_ref[0] + theirs_ref[0]
    high = mine_ref[1] + theirs_ref[1]
    raw = jnp.where(is_low, low, high)
    ends = jnp.where(is_low, mine_ref[2] + theirs_ref[2], mine_ref[3] + theirs_ref[3])
    full[0] = low
    full[1] = high
    low_first, low_last = full[0, pl.ds(0, 8, stride=4), :], full[0, pl.ds(3, 8, stride=4), :]
    high_first, high_last = full[1, pl.ds(0, 8, stride=4), :], full[1, pl.ds(3, 8, stride=4), :]
    edge_ref[...] = jnp.where(is_low, low_first, high_last)
    framed[0:8] = jnp.zeros((8, 128), jnp.float32)
    framed[8:40] = raw
    framed[40:48] = jnp.zeros((8, 128), jnp.float32)
    lane = lax.broadcasted_iota(jnp.int32, (32, 128), 1)
    row = lax.broadcasted_iota(jnp.int32, (32, 128), 0)
    west = pltpu.roll(jnp.where(lane == 127, ends, raw), 1, 1)
    east = pltpu.roll(jnp.where(lane == 0, ends, raw), 127, 1)
    neighbours = framed[4:36] + framed[12:44] + west + east
    down = jnp.where(row % 4 == 0, 0.0, framed[7:39])
    up = jnp.where(row % 4 == 3, 0.0, framed[9:41])
    neighbours = neighbours + down + up
    base_ref[...] = raw + smooth_rate * (neighbours - 6.0 * raw)
    base_ref[pl.ds(0, 8, stride=4), :] += jnp.where(is_low, 0.0, smooth_rate * low_last)
    base_ref[pl.ds(3, 8, stride=4), :] += jnp.where(is_low, smooth_rate * high_first, 0.0)


def total(mine, theirs):
    f32 = jnp.float32
    return pl.pallas_call(
        total_kernel,
        out_shape=(jax.ShapeDtypeStruct((32, 128), f32), jax.ShapeDtypeStruct((8, 128), f32)),
        scratch_shapes=[pltpu.VMEM((2, 32, 128), f32), pltpu.VMEM((48, 128), f32)],
        compiler_params=GRANT,
        name="total",
    )(mine, theirs)


def smooth_kernel(base_ref, outer_ref, out_ref):
    is_low = lax.axis_index("mer_2") == 0
    outer = smooth_rate * outer_ref[...]
    out_ref[...] = base_ref[...]
    out_ref[pl.ds(0, 8, stride=4), :] += jnp.where(is_low, outer, 0.0)
    out_ref[pl.ds(3, 8, stride=4), :] += jnp.where(is_low, 0.0, outer)


def smooth(base, outer):
    return pl.pallas_call(
        smooth_kernel,
        out_shape=jax.ShapeDtypeStruct((32, 128), jnp.float32),
        compiler_params=GRANT,
        name="smooth",
    )(base, outer)


def on_device(
    displacement,
    velocity,
    modulus,
    hoop_strength,
    coupling,
    density,
    order_count,
    point_element,
    point_local,
    azimuth_scale,
    point_owner,
    point_cell,
    adjoint_strain,
):
    count = lax.axis_size(MER)
    az_count = lax.axis_size("az")
    swap = [(0, 1), (1, 0)]
    cross = [(c, c + 1) for c in range(1, count - 1, 2)] + [(c + 1, c) for c in range(1, count - 1, 2)]
    diagonal = [(c, c - 2) for c in range(2, count, 2)] + [(c, c + 2) for c in range(1, count - 2, 2)]
    ahead = [(i, (i + 1) % az_count) for i in range(az_count)]

    own, side, points = pack(
        displacement.reshape(15, 8, 128), velocity.reshape(15, 8, 128),
        modulus, hoop_strength, coupling, density, order_count,
        point_element.T, point_local.T, azimuth_scale.reshape(1, 64), point_owner.reshape(1, 64),
        point_cell.reshape(1, 64),
    )
    sib = lax.ppermute(own, "mer_2", swap)
    same = lax.ppermute(side, MER, diagonal)
    outer = lax.ppermute(chip_message(own, sib), MER, cross)
    final, spread = march(own, sib, outer, same)

    weights = point_weights(points)
    nodes = lax.all_to_all(spread, "az", 0, 0, tiled=True)
    outgoing = messages(nodes, *weights)
    arrived = lax.all_to_all(outgoing.reshape(64, ROWS, 1, 128), SIDES, 0, 0, tiled=True)
    arrived = arrived.reshape(64 * ROWS, 128)

    adjoint = adjoint_strain.reshape(9, 32, 128)
    adjoint_sib = lax.ppermute(adjoint, "mer_2", swap)
    first, last = rims(adjoint, adjoint_sib)
    before = lax.ppermute(last, "az", ahead)
    after = lax.ppermute(first, "az", [(b, a) for a, b in ahead])
    part = voxels(arrived, adjoint, adjoint_sib, before, after)
    base, edge = total(part, lax.ppermute(part, "mer_2", swap))
    kernel = smooth(base, lax.ppermute(edge, MER, cross))
    return final.reshape(3, 5, 8, 128), kernel.reshape(8, 4, 128)


def solution(mesh):
    torus = Mesh(mesh.devices.reshape(8, 8, 2, mesh.shape["az"]), ("mer_0", "mer_1", "mer_2", "az"))
    return jax.shard_map(
        on_device,
        mesh=torus,
        in_specs=(
            P(None, None, MER, "az"),
            P(None, None, MER, "az"),
            P(None, MER),
            P(None, MER),
            P(None, MER),
            P(None, MER),
            P(None, MER),
            P(MER, None),
            P(MER, None),
            P(MER),
            P(MER, None),
            P(MER),
            P(None, None, MER, "az"),
        ),
        out_specs=(P(None, None, MER, "az"), P(None, MER, "az")),
        check_vma=False,
    )
```

```python
import math

import jax
import jax.numpy as jnp
import numpy as np
from jax import lax
from jax.experimental import pallas as pl
from jax.experimental.pallas import tpu as pltpu
from jax.sharding import Mesh
from jax.sharding import PartitionSpec as P

ORDERS = 256
STEPS = 3
MER = ("mer_0", "mer_1", "mer_2")
SIDES = ("mer_0", "mer_1")

GRANT = pltpu.CompilerParams(vmem_limit_bytes=16 << 20)

step_scale = 0.015
smooth_rate = 0.125


def gll_tables():
    nodes = np.array([-1.0, -math.sqrt(3.0 / 7.0), 0.0, math.sqrt(3.0 / 7.0), 1.0])
    weights = np.array([0.1, 49.0 / 90.0, 32.0 / 45.0, 49.0 / 90.0, 0.1])
    derivative = np.zeros((5, 5))
    for i in range(5):
        for j in range(5):
            if i == j:
                derivative[i, j] = sum(1.0 / (nodes[i] - nodes[l]) for l in range(5) if l != i)
            else:
                scale_i = np.prod([nodes[i] - nodes[l] for l in range(5) if l != i])
                scale_j = np.prod([nodes[j] - nodes[l] for l in range(5) if l != j])
                derivative[i, j] = scale_i / (scale_j * (nodes[i] - nodes[j]))
    return nodes, weights, derivative


def stiffness_rows():
    _, weights, derivative = gll_tables()
    return (derivative.T @ np.diag(weights) @ derivative) / weights[:, None]


ROWS = 37


def basis_tables():
    k = np.arange(2 * ORDERS)
    order = k // 2
    j = np.zeros(256, np.int64)
    j[:128] = np.arange(128)
    edge = np.arange(128) % 32
    j[128:] = np.where(edge < 9, -1, np.where(edge < 18, 128, 0))
    angle = (order[:, None] * j[None, :] % (2 * ORDERS)) * (2.0 * math.pi / (2 * ORDERS))
    even = (k % 2 == 0)[:, None]
    value = np.where(even, np.cos(angle), np.sin(angle))
    slope = np.where(even, -np.sin(angle), np.cos(angle))
    return (np.stack([value, slope]) / math.sqrt(ORDERS)).astype(np.float32)


def lane_tables():
    nodes = gll_tables()[0]
    rows = np.zeros((16, 256), np.float32)
    for r in range(135):
        if r < 120:
            s, a, c = r // 40, r // 8 % 5, r % 8
        else:
            s, a, c = (r - 120) // 5, (r - 120) % 5, 8

        def place(first, n):
            others = [l for l in range(5) if l != n]
            for i, l in enumerate(others):
                rows[first + i, r] = nodes[l]
            rows[first + 4, r] = 1.0 / np.prod([nodes[n] - nodes[l] for l in others])

        place(0, a)
        if c <= 4:
            place(5, c)
        if c >= 4:
            place(10, c - 4)
        rows[15, r] = s + 1
    return rows


def constant_table():
    return np.concatenate([basis_tables().reshape(1024, 256), lane_tables()], axis=0)


def split(x):
    high = x.astype(jnp.bfloat16)
    low = (x - high.astype(jnp.float32)).astype(jnp.bfloat16)
    return high, low


def dot(a, b):
    return jnp.dot(a, b, preferred_element_type=jnp.float32)


def fetch(pairs, arrived):
    copies = [pltpu.make_async_copy(a, b, arrived.at[i]) for i, (a, b) in enumerate(pairs)]
    for copy in copies:
        copy.start()
    return copies


def pack_kernel(*refs):
    sources, (own_ref, near_ref, points_ref) = refs[:12], refs[12:15]
    scratch, arrived = refs[15:27], refs[27]
    copies = fetch(list(zip(sources, scratch)), arrived)
    u_ref, v_ref = scratch[:2]
    element_ref, local_ref, scale_ref, owner_ref, cell_ref = scratch[7:]
    f32 = jnp.float32
    own_ref[30:32] = jnp.zeros((2, 8, 128), f32)
    points_ref[...] = jnp.zeros((8, 128), f32)
    for copy in copies:
        copy.wait()
    for i in range(15):
        own_ref[i] = u_ref[i]
        own_ref[15 + i] = v_ref[i]
    for i, ref in enumerate(scratch[2:7]):
        both = ref[...].astype(f32)
        own_ref[30, i:i + 1, :] = jnp.broadcast_to(both[:, 0:1], (1, 128))
        own_ref[31, i:i + 1, :] = jnp.broadcast_to(both[:, 1:2], (1, 128))
    near_columns(near_ref, own_ref, lax.axis_index("mer_2") == 1)
    points_ref[0:2, 0:64] = local_ref[...]
    points_ref[2:3, 0:64] = (element_ref[1:2, :] % 2).astype(f32)
    points_ref[3:4, 0:64] = scale_ref[...]
    points_ref[4:5, 0:64] = owner_ref[...].astype(f32)
    points_ref[5:6, 0:64] = (cell_ref[...] + 1).astype(f32)


def pack(*arrays):
    f32 = jnp.float32
    hbm, vmem = pl.BlockSpec(memory_space=pltpu.HBM), pl.BlockSpec(memory_space=pltpu.VMEM)
    return pl.pallas_call(
        pack_kernel,
        in_specs=[hbm] * 12,
        out_specs=(vmem, vmem, vmem),
        scratch_shapes=[pltpu.VMEM(a.shape, a.dtype) for a in arrays] + [pltpu.SemaphoreType.DMA((12,))],
        out_shape=(
            jax.ShapeDtypeStruct((32, 8, 128), f32),
            jax.ShapeDtypeStruct((16, 8, 128), f32),
            jax.ShapeDtypeStruct((8, 128), f32),
        ),
        name="pack",
    )(*arrays)


def near_columns(target, source, upward):
    row = lax.broadcasted_iota(jnp.int32, (8, 128), 0)
    for i in range(15):
        u, v = source[i], source[15 + i]
        start = jnp.broadcast_to(v[0:1, :], (8, 128))
        target[i] = jnp.where((row == 5) & jnp.logical_not(upward), start, u)
    target[15] = jnp.where(upward, source[31], source[30])


def stage_kernel(own_ref, out_ref):
    out_ref[0:32] = own_ref[...]
    out_ref[32:48] = jnp.zeros((16, 8, 128), jnp.float32)


def stage(own):
    return pl.pallas_call(
        stage_kernel, out_shape=jax.ShapeDtypeStruct((48, 8, 128), jnp.float32), compiler_params=GRANT,
        cost_estimate=pl.CostEstimate(flops=0, bytes_accessed=1 << 20, transcendentals=0), name="stage",
    )(own)


def chip_kernel(staged_ref, sib_ref, out_ref):
    near_columns(out_ref.at[32:48], sib_ref, lax.axis_index("mer_2") == 1)


def chip_message(staged, sib):
    return pl.pallas_call(
        chip_kernel, out_shape=jax.ShapeDtypeStruct((48, 8, 128), jnp.float32),
        input_output_aliases={0: 0}, compiler_params=GRANT, name="chip",
    )(staged, sib)


def step_kernel(own_ref, sib_ref, cross_ref, diagonal_ref, u_ref, gather_ref,
                ucol, vcol, coef, state, field):
    core, az = lax.axis_index("mer_2"), lax.axis_index("az")
    is_low = core == 0

    def left(i):
        return jnp.where(is_low, cross_ref[i], sib_ref[i])

    def right(i):
        return jnp.where(is_low, sib_ref[i], cross_ref[i])

    def far_left(i):
        return jnp.where(is_low, cross_ref[32 + i], diagonal_ref[i])

    def far_right(i):
        return jnp.where(is_low, diagonal_ref[i], cross_ref[32 + i])

    zero8 = jnp.zeros((8, 128), jnp.float32)
    for i in range(15):
        ucol[i, 0:8, :] = far_left(i)
        ucol[i, 8:16, :] = left(i)
        ucol[i, 16:24, :] = own_ref[i]
        ucol[i, 24:32, :] = right(i)
        high = far_right(i)
        ucol[i, 32:40, :] = high
        vcol[i, 0:8, :] = zero8
        vcol[i, 8:16, :] = left(15 + i)
        vcol[i, 16:24, :] = own_ref[15 + i]
        vcol[i, 24:32, :] = right(15 + i)
        vcol[i, 32:40, :] = zero8
        vcol[i, 32:33, :] = high[5:6, :]
    l0, l1, r0, r1 = left(30), left(31), right(30), right(31)
    sources = (far_left(15), l0, l1, own_ref[30], own_ref[31], r0, r1, far_right(15))
    for i in range(5):
        for e, tile in enumerate(sources):
            coef[i, e:e + 1, :] = tile[i:i + 1, :]

    lane = lax.broadcasted_iota(jnp.int32, (8, 128), 1)
    order = ((az * 128 + lane) // 2).astype(jnp.float32)
    ratio = order * (1.0 / ORDERS)
    mask = jnp.where(order < coef[4], 1.0, 0.0)
    is_even = lane % 2 == 0
    stiff = coef[0] * mask
    hoop = coef[1] * mask * ratio * ratio
    couple = coef[2] * mask * ratio
    couple_even = jnp.where(is_even, couple, 0.0)
    couple_odd = jnp.where(is_even, 0.0, -couple)
    density = coef[3]
    present = density > 0.0
    inner = jnp.where(present, step_scale / jnp.where(present, density, 1.0), 0.0)
    shared_density = density + pltpu.roll(density, 1, 0)
    edge = jnp.where(present, step_scale / jnp.where(present, shared_density, 1.0), 0.0)
    field[0], field[1], field[2], field[3], field[4], field[5] = (
        stiff, hoop, couple_even, couple_odd, inner, edge)

    for i in range(15):
        for b in range(5):
            u = ucol[i, pl.ds(4 + b, 8, stride=4), :]
            state[0, i, b] = u
            if b < 4:
                state[1, i, b] = u - vcol[i, pl.ds(4 + b, 8, stride=4), :]

    rows = stiffness_rows()

    def one_step(n, carry):
        now = lax.rem(n, 2)
        other = 1 - now
        stiff, hoop = field[0], field[1]
        couple_even, couple_odd = field[2], field[3]
        inner, edge = field[4], field[5]

        def coupled(x):
            return pltpu.roll(x, 127, 1) * couple_even + pltpu.roll(x, 1, 1) * couple_odd

        for s in range(3):
            u = [[state[now, 5 * s + a, b] for b in range(5)] for a in range(5)]
            for a in range(5):
                forces = []
                for b in range(5):
                    total = u[a][b] * float(rows[a, a] + rows[b, b])
                    for other_a in range(5):
                        if other_a != a:
                            total = total + u[other_a][b] * float(rows[a, other_a])
                    for other_b in range(5):
                        if other_b != b:
                            total = total + u[a][other_b] * float(rows[b, other_b])
                    force = -(stiff * total + hoop * u[a][b])
                    if s == 0:
                        force = force + coupled(state[now, 10 + a, b])
                    if s == 2:
                        force = force - coupled(state[now, a, b])
                    forces.append(force)
                forces[0] = forces[0] + pltpu.roll(forces[4], 1, 0)
                for b in range(4):
                    following = (
                        2.0 * u[a][b] - state[other, 5 * s + a, b]
                        + (edge if b == 0 else inner) * forces[b]
                    )
                    state[other, 5 * s + a, b] = following
                    if b == 0:
                        state[other, 5 * s + a, 4] = pltpu.roll(following, 7, 0)
        return carry

    lax.fori_loop(0, STEPS, one_step, 0)
    last = STEPS % 2
    for i in range(15):
        for b in range(4):
            ucol[i, pl.ds(4 + b, 8, stride=4), :] = state[last, i, b]
    for q in range(4):
        gather_ref[q, 15:17] = jnp.zeros((2, 8, 128), jnp.float32)
    for i in range(15):
        own = ucol[i, 16:24, :]
        rim = ucol[i, 24:25, :]
        u_ref[i] = own
        for q in range(4):
            gather_ref[q, i] = own
            gather_ref[q, 15 + i // 8, i % 8:i % 8 + 1, :] = rim


def march(own, sib, cross, diagonal):
    f32 = jnp.float32
    vmem = pl.BlockSpec(memory_space=pltpu.VMEM)
    return pl.pallas_call(
        step_kernel,
        in_specs=[vmem] * 4,
        out_specs=(vmem, vmem),
        out_shape=(
            jax.ShapeDtypeStruct((15, 8, 128), f32),
            jax.ShapeDtypeStruct((4, 17, 8, 128), f32),
        ),
        scratch_shapes=[
            pltpu.VMEM((15, 40, 128), f32),
            pltpu.VMEM((15, 40, 128), f32),
            pltpu.VMEM((5, 8, 128), f32),
            pltpu.VMEM((2, 15, 5, 8, 128), f32),
            pltpu.VMEM((6, 8, 128), f32),
        ],
        compiler_params=GRANT,
        name="march",
    )(own, sib, cross, diagonal)


def weight_kernel(points_ref, table_ref, weight_ref, point_ref, basis_ref):
    f32, bf16 = jnp.float32, jnp.bfloat16
    az = lax.axis_index("az")
    diagonal = (lax.broadcasted_iota(jnp.int32, (64, 128), 0)
                == lax.broadcasted_iota(jnp.int32, (64, 128), 1))

    def upright(line):
        return jnp.sum(jnp.where(diagonal, line, 0.0), axis=1, keepdims=True)

    xi, eta, second, scale, owner, code = (upright(points_ref[i:i + 1, :]) for i in range(6))

    def basis(x, rows):
        d1, d2, d3, d4 = x - rows[0], x - rows[1], x - rows[2], x - rows[3]
        d12, d34 = d1 * d2, d3 * d4
        return d12 * d34 * rows[4], ((d1 + d2) * d34 + d12 * (d3 + d4)) * rows[4]

    lanes = [table_ref[1024 + i:1025 + i, :] for i in range(16)]
    value_a, slope_a = basis(xi, lanes[0:5])
    first_b = basis(eta, lanes[5:10])
    second_b = basis(eta, lanes[10:15])
    value_b = jnp.where(second > 0.5, second_b[0], first_b[0])
    slope_b = jnp.where(second > 0.5, second_b[1], first_b[1])
    around = value_a * value_b * scale
    point = split(jnp.concatenate([slope_a * value_b, value_a * slope_b, around], axis=0))
    point_ref[0, 0:192] = point[0]
    point_ref[1, 0:192] = point[1]

    lane = lax.broadcasted_iota(jnp.int32, (64, 128), 1)
    sub = lax.broadcasted_iota(jnp.int32, (64, 128), 0)
    owners = points_ref[4:5, :]
    rank = jnp.sum(jnp.where((owner == owners) & (sub < lane), 1.0, 0.0), axis=0, keepdims=True)
    slot = owners * 2.0 + rank
    row = lax.broadcasted_iota(jnp.int32, (256, 128), 0)
    column = lax.broadcasted_iota(jnp.int32, (256, 128), 1)
    row_slot = (row % 64) * 4 + row // 64
    place = jnp.where((slot == row_slot.astype(f32)) & (column < 64), 1.0, 0.0).astype(bf16)[:, :64]
    for n in range(2):
        for d in range(3):
            weight_ref[2 * d + n] = dot(place, point[n][64 * d:64 * d + 64]).astype(bf16)

    upright_slot = upright(slot)
    group = (lane // 32).astype(f32)
    mine = upright_slot - 4.0 * jnp.floor(upright_slot * 0.25) == group
    point_ref[0, 192:256, 0:128] = jnp.where(mine & (lane % 32 == 31), code, 0.0).astype(bf16)
    point_ref[0, 192:256, 128:256] = jnp.where(mine & (lane % 32 < 18), 1.0, 0.0).astype(bf16)
    chip = jnp.where((jnp.floor(slot * 0.25) == sub.astype(f32)) & (lane < 64), 1.0, 0.0).astype(bf16)
    point_ref[1, 192:256, 0:128] = chip
    point_ref[1, 192:256, 128:256] = chip

    order = lax.broadcasted_iota(jnp.int32, (512, 128), 0) // 2
    turns = (order * az) % 4
    along = jnp.where(turns == 0, 1.0, jnp.where(turns == 2, -1.0, 0.0))
    across = jnp.where(turns == 1, 1.0, jnp.where(turns == 3, -1.0, 0.0))
    ratio = order.astype(f32) * (1.0 / ORDERS)
    first, other = slice(0, 512), slice(512, 1024)
    low_lanes, edge_lanes = slice(0, 128), slice(128, 256)
    value = along * table_ref[first, low_lanes] + across * table_ref[other, low_lanes]
    slope = ratio * (along * table_ref[other, low_lanes] - across * table_ref[first, low_lanes])
    edge_value = along * table_ref[first, edge_lanes] + across * table_ref[other, edge_lanes]
    edge_slope = ratio * (along * table_ref[other, edge_lanes] - across * table_ref[first, edge_lanes])
    kind = ((lax.broadcasted_iota(jnp.int32, (512, 128), 1) % 32) % 9) % 3
    edge = jnp.where(kind == 2, edge_slope, edge_value)
    for i, block in enumerate((value, slope, edge)):
        high, low = split(block)
        basis_ref[0, :, 128 * i:128 * i + 128] = high
        basis_ref[1, :, 128 * i:128 * i + 128] = low


def point_weights(points):
    bf16 = jnp.bfloat16
    return pl.pallas_call(
        weight_kernel,
        out_shape=(
            jax.ShapeDtypeStruct((6, 256, 256), bf16),
            jax.ShapeDtypeStruct((2, 256, 256), bf16),
            jax.ShapeDtypeStruct((2, 512, 384), bf16),
        ),
        compiler_params=GRANT,
        name="weights",
    )(points, jnp.asarray(constant_table()))


def thrice(a, b):
    return dot(a[0], b[0]) + (dot(a[1], b[0]) + dot(a[0], b[1]))


def message_kernel(nodes_ref, weight_ref, point_ref, basis_ref, out_ref):
    f32 = jnp.float32
    coefs = jnp.concatenate([nodes_ref[q].reshape(136, 128) for q in range(4)], axis=1)
    samples = thrice(split(coefs), (basis_ref[0], basis_ref[1]))
    row = lax.broadcasted_iota(jnp.int32, (136, 128), 0)
    component = jnp.where(row < 120, row // 40, (row - 120) // 5)
    pad = jnp.zeros((120, 384), f32)
    values, slopes, edges = samples[:, :128], samples[:, 128:256], samples[:, 256:]

    def spread(block):
        parts = jnp.concatenate([jnp.where(component == s, block, 0.0) for s in range(3)], axis=1)
        return split(jnp.concatenate([parts, pad], axis=0))

    by_kind = (spread(values), None, spread(slopes))
    for d in range(3):
        field = by_kind[0] if d < 2 else by_kind[2]
        rows = thrice((weight_ref[2 * d], weight_ref[2 * d + 1]), field)
        for s in range(3):
            for c in range(4):
                out_ref[pl.ds(4 * (3 * s + d) + c, 64, stride=ROWS), :] = (
                    rows[64 * c:64 * c + 64, 128 * s:128 * s + 128])

    lane = lax.broadcasted_iota(jnp.int32, (136, 128), 1)
    edges = jnp.where(((lane % 32) % 9) // 3 == component, edges, 0.0)
    edges = split(jnp.concatenate([edges, pad[:, :128]], axis=0))
    rows = thrice((point_ref[0, 0:192], point_ref[1, 0:192]), edges)
    lane = lax.broadcasted_iota(jnp.int32, (64, 128), 1)
    kind = ((lane % 32) % 9) % 3
    extra = jnp.where(kind == 0, rows[:64], jnp.where(kind == 1, rows[64:128], rows[128:]))
    extra = (extra * point_ref[0, 192:256, 128:256].astype(f32)
             + point_ref[0, 192:256, 0:128].astype(f32))
    chip = point_ref[1, 192:256, 0:64]
    high, low = split(extra)
    out_ref[pl.ds(36, 64, stride=ROWS), :] = dot(chip, high) + dot(chip, low)


def messages(nodes, *weights):
    return pl.pallas_call(
        message_kernel,
        out_shape=jax.ShapeDtypeStruct((64 * ROWS, 128), jnp.float32),
        compiler_params=GRANT,
        name="messages",
    )(nodes, *weights)


def rims_kernel(own_ref, sib_ref, first_ref, last_ref):
    lane = lax.broadcasted_iota(jnp.int32, (32, 128), 1)
    for n, ref in enumerate((own_ref, sib_ref)):
        first = jnp.zeros((32, 128), jnp.float32)
        last = jnp.zeros((32, 128), jnp.float32)
        for g in range(9):
            first = jnp.where(lane == 9 + g, ref[g, :, 0:1], first)
            last = jnp.where(lane == g, ref[g, :, 127:128], last)
        first_ref[n] = first
        last_ref[n] = last


def rims(own, sib):
    shape = jax.ShapeDtypeStruct((2, 32, 128), jnp.float32)
    return pl.pallas_call(
        rims_kernel, out_shape=(shape, shape), compiler_params=GRANT, name="rims",
    )(own, sib)


def voxel_kernel(arrived_ref, own_ref, sib_ref, before_ref, after_ref, out_ref):
    is_low = lax.axis_index("mer_2") == 0
    f32 = jnp.float32
    tail = arrived_ref[pl.ds(36, 64, stride=ROWS), :]
    lane = lax.broadcasted_iota(jnp.int32, (64, 128), 1)
    wanted = (lane % 32 + 1).astype(f32)
    sorting = jnp.concatenate(
        [
            jnp.where((lane // 32 == c // 2) & (tail[:, 32 * c + 31:32 * c + 32] == wanted), 1.0, 0.0)
            for c in range(4)
        ],
        axis=0,
    ).astype(jnp.bfloat16)

    def sorted_sum(rows):
        high, low = split(rows)
        both = lax.dot_general(
            sorting, jnp.concatenate([high, low], axis=1), (((0,), (0,)), ((), ())),
            preferred_element_type=f32,
        )
        return both[:64, :128] + both[:64, 128:]

    totals = [jnp.zeros((32, 128), f32) for _ in range(2)]
    for g in range(9):
        summed = sorted_sum(jnp.concatenate(
            [arrived_ref[pl.ds(4 * g + c, 64, stride=ROWS), :] for c in range(4)], axis=0))
        mine, theirs = own_ref[g], sib_ref[g]
        totals[0] = totals[0] + summed[:32] * jnp.where(is_low, mine, theirs)
        totals[1] = totals[1] + summed[32:] * jnp.where(is_low, theirs, mine)
    shifted = [tail] + [pltpu.roll(tail, 128 - 32 * c, 1) for c in range(1, 4)]
    ends = sorted_sum(jnp.concatenate([jnp.where(lane < 18, x, 0.0) for x in shifted], axis=0))
    own_edge, sib_edge = before_ref[0] + after_ref[0], before_ref[1] + after_ref[1]
    side = (ends[:32] * jnp.where(is_low, own_edge, sib_edge), ends[32:] * jnp.where(is_low, sib_edge, own_edge))
    out_ref[0] = totals[0]
    out_ref[1] = totals[1]
    for core in range(2):
        product = side[core]
        small = lax.broadcasted_iota(jnp.int32, (32, 128), 1)
        west = jnp.sum(jnp.where(small < 9, product, 0.0), axis=1, keepdims=True)
        east = jnp.sum(jnp.where((small >= 9) & (small < 18), product, 0.0), axis=1, keepdims=True)
        out_ref[2 + core] = jnp.where(small == 127, west, jnp.where(small == 0, east, 0.0))


def voxels(arrived, own, sib, before, after):
    f32 = jnp.float32
    return pl.pallas_call(
        voxel_kernel,
        out_shape=jax.ShapeDtypeStruct((4, 32, 128), f32),
        compiler_params=GRANT,
        name="voxels",
    )(arrived, own, sib, before, after)


def total_kernel(mine_ref, theirs_ref, base_ref, edge_ref, full, framed):
    is_low = lax.axis_index("mer_2") == 0
    low = mine_ref[0] + theirs_ref[0]
    high = mine_ref[1] + theirs_ref[1]
    raw = jnp.where(is_low, low, high)
    ends = jnp.where(is_low, mine_ref[2] + theirs_ref[2], mine_ref[3] + theirs_ref[3])
    full[0] = low
    full[1] = high
    low_first, low_last = full[0, pl.ds(0, 8, stride=4), :], full[0, pl.ds(3, 8, stride=4), :]
    high_first, high_last = full[1, pl.ds(0, 8, stride=4), :], full[1, pl.ds(3, 8, stride=4), :]
    edge_ref[...] = jnp.where(is_low, low_first, high_last)
    framed[0:8] = jnp.zeros((8, 128), jnp.float32)
    framed[8:40] = raw
    framed[40:48] = jnp.zeros((8, 128), jnp.float32)
    lane = lax.broadcasted_iota(jnp.int32, (32, 128), 1)
    row = lax.broadcasted_iota(jnp.int32, (32, 128), 0)
    west = pltpu.roll(jnp.where(lane == 127, ends, raw), 1, 1)
    east = pltpu.roll(jnp.where(lane == 0, ends, raw), 127, 1)
    neighbours = framed[4:36] + framed[12:44] + west + east
    down = jnp.where(row % 4 == 0, 0.0, framed[7:39])
    up = jnp.where(row % 4 == 3, 0.0, framed[9:41])
    neighbours = neighbours + down + up
    base_ref[...] = raw + smooth_rate * (neighbours - 6.0 * raw)
    base_ref[pl.ds(0, 8, stride=4), :] += jnp.where(is_low, 0.0, smooth_rate * low_last)
    base_ref[pl.ds(3, 8, stride=4), :] += jnp.where(is_low, smooth_rate * high_first, 0.0)


def total(mine, theirs):
    f32 = jnp.float32
    return pl.pallas_call(
        total_kernel,
        out_shape=(jax.ShapeDtypeStruct((32, 128), f32), jax.ShapeDtypeStruct((8, 128), f32)),
        scratch_shapes=[pltpu.VMEM((2, 32, 128), f32), pltpu.VMEM((48, 128), f32)],
        compiler_params=GRANT,
        name="total",
    )(mine, theirs)


def smooth_kernel(base_ref, outer_ref, out_ref):
    is_low = lax.axis_index("mer_2") == 0
    outer = smooth_rate * outer_ref[...]
    out_ref[...] = base_ref[...]
    out_ref[pl.ds(0, 8, stride=4), :] += jnp.where(is_low, outer, 0.0)
    out_ref[pl.ds(3, 8, stride=4), :] += jnp.where(is_low, 0.0, outer)


def smooth(base, outer):
    return pl.pallas_call(
        smooth_kernel,
        out_shape=jax.ShapeDtypeStruct((32, 128), jnp.float32),
        compiler_params=GRANT,
        name="smooth",
    )(base, outer)


def on_device(
    displacement,
    velocity,
    modulus,
    hoop_strength,
    coupling,
    density,
    order_count,
    point_element,
    point_local,
    azimuth_scale,
    point_owner,
    point_cell,
    adjoint_strain,
):
    count = lax.axis_size(MER)
    az_count = lax.axis_size("az")
    swap = [(0, 1), (1, 0)]
    cross = [(c, c + 1) for c in range(1, count - 1, 2)] + [(c + 1, c) for c in range(1, count - 1, 2)]
    diagonal = [(c, c - 2) for c in range(2, count, 2)] + [(c, c + 2) for c in range(1, count - 2, 2)]
    ahead = [(i, (i + 1) % az_count) for i in range(az_count)]

    own, side, points = pack(
        displacement.reshape(15, 8, 128), velocity.reshape(15, 8, 128),
        modulus, hoop_strength, coupling, density, order_count,
        point_element.T, point_local.T, azimuth_scale.reshape(1, 64), point_owner.reshape(1, 64),
        point_cell.reshape(1, 64),
    )
    sib = lax.ppermute(own, "mer_2", swap)
    same = lax.ppermute(side, MER, diagonal)
    message = chip_message(stage(own), sib)
    outer = lax.ppermute(message, MER, cross)
    final, spread = march(message, sib, outer, same)

    weights = point_weights(points)
    nodes = lax.all_to_all(spread, "az", 0, 0, tiled=True)
    outgoing = messages(nodes, *weights)
    arrived = lax.all_to_all(outgoing.reshape(64, ROWS, 1, 128), SIDES, 0, 0, tiled=True)
    arrived = arrived.reshape(64 * ROWS, 128)

    adjoint = adjoint_strain.reshape(9, 32, 128)
    adjoint_sib = lax.ppermute(adjoint, "mer_2", swap)
    first, last = rims(adjoint, adjoint_sib)
    before = lax.ppermute(last, "az", ahead)
    after = lax.ppermute(first, "az", [(b, a) for a, b in ahead])
    part = voxels(arrived, adjoint, adjoint_sib, before, after)
    base, edge = total(part, lax.ppermute(part, "mer_2", swap))
    kernel = smooth(base, lax.ppermute(edge, MER, cross))
    return final.reshape(3, 5, 8, 128), kernel.reshape(8, 4, 128)


def solution(mesh):
    torus = Mesh(mesh.devices.reshape(8, 8, 2, mesh.shape["az"]), ("mer_0", "mer_1", "mer_2", "az"))
    return jax.shard_map(
        on_device,
        mesh=torus,
        in_specs=(
            P(None, None, MER, "az"),
            P(None, None, MER, "az"),
            P(None, MER),
            P(None, MER),
            P(None, MER),
            P(None, MER),
            P(None, MER),
            P(MER, None),
            P(MER, None),
            P(MER),
            P(MER, None),
            P(MER),
            P(None, None, MER, "az"),
        ),
        out_specs=(P(None, None, MER, "az"), P(None, MER, "az")),
        check_vma=False,
    )
```

```python
import math

import jax
import jax.numpy as jnp
import numpy as np
from jax import lax
from jax.experimental import pallas as pl
from jax.experimental.pallas import tpu as pltpu
from jax.sharding import Mesh
from jax.sharding import PartitionSpec as P

ORDERS = 256
STEPS = 3
MER = ("mer_0", "mer_1", "mer_2")
SIDES = ("mer_0", "mer_1")

GRANT = pltpu.CompilerParams(vmem_limit_bytes=16 << 20)

step_scale = 0.015
smooth_rate = 0.125


def gll_tables():
    nodes = np.array([-1.0, -math.sqrt(3.0 / 7.0), 0.0, math.sqrt(3.0 / 7.0), 1.0])
    weights = np.array([0.1, 49.0 / 90.0, 32.0 / 45.0, 49.0 / 90.0, 0.1])
    derivative = np.zeros((5, 5))
    for i in range(5):
        for j in range(5):
            if i == j:
                derivative[i, j] = sum(1.0 / (nodes[i] - nodes[l]) for l in range(5) if l != i)
            else:
                scale_i = np.prod([nodes[i] - nodes[l] for l in range(5) if l != i])
                scale_j = np.prod([nodes[j] - nodes[l] for l in range(5) if l != j])
                derivative[i, j] = scale_i / (scale_j * (nodes[i] - nodes[j]))
    return nodes, weights, derivative


def stiffness_rows():
    _, weights, derivative = gll_tables()
    return (derivative.T @ np.diag(weights) @ derivative) / weights[:, None]


ROWS = 37


def basis_tables():
    k = np.arange(2 * ORDERS)
    order = k // 2
    j = np.zeros(256, np.int64)
    j[:128] = np.arange(128)
    edge = np.arange(128) % 32
    j[128:] = np.where(edge < 9, -1, np.where(edge < 18, 128, 0))
    angle = (order[:, None] * j[None, :] % (2 * ORDERS)) * (2.0 * math.pi / (2 * ORDERS))
    even = (k % 2 == 0)[:, None]
    value = np.where(even, np.cos(angle), np.sin(angle))
    slope = np.where(even, -np.sin(angle), np.cos(angle))
    return (np.stack([value, slope]) / math.sqrt(ORDERS)).astype(np.float32)


def lane_tables():
    nodes = gll_tables()[0]
    rows = np.zeros((16, 256), np.float32)
    for r in range(135):
        if r < 120:
            s, a, c = r // 40, r // 8 % 5, r % 8
        else:
            s, a, c = (r - 120) // 5, (r - 120) % 5, 8

        def place(first, n):
            others = [l for l in range(5) if l != n]
            for i, l in enumerate(others):
                rows[first + i, r] = nodes[l]
            rows[first + 4, r] = 1.0 / np.prod([nodes[n] - nodes[l] for l in others])

        place(0, a)
        if c <= 4:
            place(5, c)
        if c >= 4:
            place(10, c - 4)
        rows[15, r] = s + 1
    return rows


def constant_table():
    return np.concatenate([basis_tables().reshape(1024, 256), lane_tables()], axis=0)


def split(x):
    high = x.astype(jnp.bfloat16)
    low = (x - high.astype(jnp.float32)).astype(jnp.bfloat16)
    return high, low


def dot(a, b):
    return jnp.dot(a, b, preferred_element_type=jnp.float32)


def fetch(pairs, arrived):
    copies = [pltpu.make_async_copy(a, b, arrived.at[i]) for i, (a, b) in enumerate(pairs)]
    for copy in copies:
        copy.start()
    return copies


def pack_kernel(*refs):
    sources, (own_ref, points_ref) = refs[:12], refs[12:14]
    scratch, arrived = refs[14:26], refs[26]
    copies = fetch(list(zip(sources, scratch)), arrived)
    u_ref, v_ref = scratch[:2]
    element_ref, local_ref, scale_ref, owner_ref, cell_ref = scratch[7:]
    f32 = jnp.float32
    own_ref[30:32] = jnp.zeros((2, 8, 128), f32)
    points_ref[...] = jnp.zeros((8, 128), f32)
    for copy in copies:
        copy.wait()
    for i in range(15):
        own_ref[i] = u_ref[i]
        own_ref[15 + i] = v_ref[i]
    for i, ref in enumerate(scratch[2:7]):
        both = ref[...].astype(f32)
        own_ref[30, i:i + 1, :] = jnp.broadcast_to(both[:, 0:1], (1, 128))
        own_ref[31, i:i + 1, :] = jnp.broadcast_to(both[:, 1:2], (1, 128))
    points_ref[0:2, 0:64] = local_ref[...]
    points_ref[2:3, 0:64] = (element_ref[1:2, :] % 2).astype(f32)
    points_ref[3:4, 0:64] = scale_ref[...]
    points_ref[4:5, 0:64] = owner_ref[...].astype(f32)
    points_ref[5:6, 0:64] = (cell_ref[...] + 1).astype(f32)


def pack(*arrays):
    f32 = jnp.float32
    hbm, vmem = pl.BlockSpec(memory_space=pltpu.HBM), pl.BlockSpec(memory_space=pltpu.VMEM)
    return pl.pallas_call(
        pack_kernel,
        in_specs=[hbm] * 12,
        out_specs=(vmem, vmem),
        scratch_shapes=[pltpu.VMEM(a.shape, a.dtype) for a in arrays] + [pltpu.SemaphoreType.DMA((12,))],
        out_shape=(
            jax.ShapeDtypeStruct((32, 8, 128), f32),
            jax.ShapeDtypeStruct((8, 128), f32),
        ),
        name="pack",
    )(*arrays)


def near_columns(target, source, upward):
    row = lax.broadcasted_iota(jnp.int32, (8, 128), 0)
    for i in range(15):
        u, v = source[i], source[15 + i]
        start = jnp.broadcast_to(v[0:1, :], (8, 128))
        target[i] = jnp.where((row == 5) & jnp.logical_not(upward), start, u)
    target[15] = jnp.where(upward, source[31], source[30])


def stage_kernel(own_ref, out_ref, side_ref):
    near_columns(side_ref, own_ref, lax.axis_index("mer_2") == 1)
    out_ref[0:32] = own_ref[...]
    out_ref[32:48] = jnp.zeros((16, 8, 128), jnp.float32)


def stage(own):
    return pl.pallas_call(
        stage_kernel, compiler_params=GRANT,
        out_shape=(
            jax.ShapeDtypeStruct((48, 8, 128), jnp.float32), jax.ShapeDtypeStruct((16, 8, 128), jnp.float32)),
        cost_estimate=pl.CostEstimate(flops=0, bytes_accessed=1 << 20, transcendentals=0), name="stage",
    )(own)


def chip_kernel(staged_ref, sib_ref, out_ref):
    near_columns(out_ref.at[32:48], sib_ref, lax.axis_index("mer_2") == 1)


def chip_message(staged, sib):
    return pl.pallas_call(
        chip_kernel, out_shape=jax.ShapeDtypeStruct((48, 8, 128), jnp.float32),
        input_output_aliases={0: 0}, compiler_params=GRANT, name="chip",
    )(staged, sib)


def step_kernel(own_ref, sib_ref, cross_ref, diagonal_ref, u_ref, gather_ref,
                ucol, vcol, coef, state, field):
    core, az = lax.axis_index("mer_2"), lax.axis_index("az")
    is_low = core == 0

    def left(i):
        return jnp.where(is_low, cross_ref[i], sib_ref[i])

    def right(i):
        return jnp.where(is_low, sib_ref[i], cross_ref[i])

    def far_left(i):
        return jnp.where(is_low, cross_ref[32 + i], diagonal_ref[i])

    def far_right(i):
        return jnp.where(is_low, diagonal_ref[i], cross_ref[32 + i])

    zero8 = jnp.zeros((8, 128), jnp.float32)
    for i in range(15):
        ucol[i, 0:8, :] = far_left(i)
        ucol[i, 8:16, :] = left(i)
        ucol[i, 16:24, :] = own_ref[i]
        ucol[i, 24:32, :] = right(i)
        high = far_right(i)
        ucol[i, 32:40, :] = high
        vcol[i, 0:8, :] = zero8
        vcol[i, 8:16, :] = left(15 + i)
        vcol[i, 16:24, :] = own_ref[15 + i]
        vcol[i, 24:32, :] = right(15 + i)
        vcol[i, 32:40, :] = zero8
        vcol[i, 32:33, :] = high[5:6, :]
    l0, l1, r0, r1 = left(30), left(31), right(30), right(31)
    sources = (far_left(15), l0, l1, own_ref[30], own_ref[31], r0, r1, far_right(15))
    for i in range(5):
        for e, tile in enumerate(sources):
            coef[i, e:e + 1, :] = tile[i:i + 1, :]

    lane = lax.broadcasted_iota(jnp.int32, (8, 128), 1)
    order = ((az * 128 + lane) // 2).astype(jnp.float32)
    ratio = order * (1.0 / ORDERS)
    mask = jnp.where(order < coef[4], 1.0, 0.0)
    is_even = lane % 2 == 0
    stiff = coef[0] * mask
    hoop = coef[1] * mask * ratio * ratio
    couple = coef[2] * mask * ratio
    couple_even = jnp.where(is_even, couple, 0.0)
    couple_odd = jnp.where(is_even, 0.0, -couple)
    density = coef[3]
    present = density > 0.0
    inner = jnp.where(present, step_scale / jnp.where(present, density, 1.0), 0.0)
    shared_density = density + pltpu.roll(density, 1, 0)
    edge = jnp.where(present, step_scale / jnp.where(present, shared_density, 1.0), 0.0)
    field[0], field[1], field[2], field[3], field[4], field[5] = (
        stiff, hoop, couple_even, couple_odd, inner, edge)

    for i in range(15):
        for b in range(5):
            u = ucol[i, pl.ds(4 + b, 8, stride=4), :]
            state[0, i, b] = u
            if b < 4:
                state[1, i, b] = u - vcol[i, pl.ds(4 + b, 8, stride=4), :]

    rows = stiffness_rows()

    def one_step(n, carry):
        now = lax.rem(n, 2)
        other = 1 - now
        stiff, hoop = field[0], field[1]
        couple_even, couple_odd = field[2], field[3]
        inner, edge = field[4], field[5]

        def coupled(x):
            return pltpu.roll(x, 127, 1) * couple_even + pltpu.roll(x, 1, 1) * couple_odd

        for s in range(3):
            u = [[state[now, 5 * s + a, b] for b in range(5)] for a in range(5)]
            for a in range(5):
                forces = []
                for b in range(5):
                    total = u[a][b] * float(rows[a, a] + rows[b, b])
                    for other_a in range(5):
                        if other_a != a:
                            total = total + u[other_a][b] * float(rows[a, other_a])
                    for other_b in range(5):
                        if other_b != b:
                            total = total + u[a][other_b] * float(rows[b, other_b])
                    force = -(stiff * total + hoop * u[a][b])
                    if s == 0:
                        force = force + coupled(state[now, 10 + a, b])
                    if s == 2:
                        force = force - coupled(state[now, a, b])
                    forces.append(force)
                forces[0] = forces[0] + pltpu.roll(forces[4], 1, 0)
                for b in range(4):
                    following = (
                        2.0 * u[a][b] - state[other, 5 * s + a, b]
                        + (edge if b == 0 else inner) * forces[b]
                    )
                    state[other, 5 * s + a, b] = following
                    if b == 0:
                        state[other, 5 * s + a, 4] = pltpu.roll(following, 7, 0)
        return carry

    lax.fori_loop(0, STEPS, one_step, 0)
    last = STEPS % 2
    for i in range(15):
        for b in range(4):
            ucol[i, pl.ds(4 + b, 8, stride=4), :] = state[last, i, b]
    for q in range(4):
        gather_ref[q, 15:17] = jnp.zeros((2, 8, 128), jnp.float32)
    for i in range(15):
        own = ucol[i, 16:24, :]
        rim = ucol[i, 24:25, :]
        u_ref[i] = own
        for q in range(4):
            gather_ref[q, i] = own
            gather_ref[q, 15 + i // 8, i % 8:i % 8 + 1, :] = rim


def march(own, sib, cross, diagonal):
    f32 = jnp.float32
    vmem = pl.BlockSpec(memory_space=pltpu.VMEM)
    return pl.pallas_call(
        step_kernel,
        in_specs=[vmem] * 4,
        out_specs=(vmem, vmem),
        out_shape=(
            jax.ShapeDtypeStruct((15, 8, 128), f32),
            jax.ShapeDtypeStruct((4, 17, 8, 128), f32),
        ),
        scratch_shapes=[
            pltpu.VMEM((15, 40, 128), f32),
            pltpu.VMEM((15, 40, 128), f32),
            pltpu.VMEM((5, 8, 128), f32),
            pltpu.VMEM((2, 15, 5, 8, 128), f32),
            pltpu.VMEM((6, 8, 128), f32),
        ],
        compiler_params=GRANT,
        name="march",
    )(own, sib, cross, diagonal)


def weight_kernel(points_ref, table_ref, weight_ref, point_ref, basis_ref):
    f32, bf16 = jnp.float32, jnp.bfloat16
    az = lax.axis_index("az")
    diagonal = (lax.broadcasted_iota(jnp.int32, (64, 128), 0)
                == lax.broadcasted_iota(jnp.int32, (64, 128), 1))

    def upright(line):
        return jnp.sum(jnp.where(diagonal, line, 0.0), axis=1, keepdims=True)

    xi, eta, second, scale, owner, code = (upright(points_ref[i:i + 1, :]) for i in range(6))

    def basis(x, rows):
        d1, d2, d3, d4 = x - rows[0], x - rows[1], x - rows[2], x - rows[3]
        d12, d34 = d1 * d2, d3 * d4
        return d12 * d34 * rows[4], ((d1 + d2) * d34 + d12 * (d3 + d4)) * rows[4]

    lanes = [table_ref[1024 + i:1025 + i, :] for i in range(16)]
    value_a, slope_a = basis(xi, lanes[0:5])
    first_b = basis(eta, lanes[5:10])
    second_b = basis(eta, lanes[10:15])
    value_b = jnp.where(second > 0.5, second_b[0], first_b[0])
    slope_b = jnp.where(second > 0.5, second_b[1], first_b[1])
    around = value_a * value_b * scale
    point = split(jnp.concatenate([slope_a * value_b, value_a * slope_b, around], axis=0))
    point_ref[0, 0:192] = point[0]
    point_ref[1, 0:192] = point[1]

    lane = lax.broadcasted_iota(jnp.int32, (64, 128), 1)
    sub = lax.broadcasted_iota(jnp.int32, (64, 128), 0)
    owners = points_ref[4:5, :]
    rank = jnp.sum(jnp.where((owner == owners) & (sub < lane), 1.0, 0.0), axis=0, keepdims=True)
    slot = owners * 2.0 + rank
    row = lax.broadcasted_iota(jnp.int32, (256, 128), 0)
    column = lax.broadcasted_iota(jnp.int32, (256, 128), 1)
    row_slot = (row % 64) * 4 + row // 64
    place = jnp.where((slot == row_slot.astype(f32)) & (column < 64), 1.0, 0.0).astype(bf16)[:, :64]
    for n in range(2):
        for d in range(3):
            weight_ref[2 * d + n] = dot(place, point[n][64 * d:64 * d + 64]).astype(bf16)

    upright_slot = upright(slot)
    group = (lane // 32).astype(f32)
    mine = upright_slot - 4.0 * jnp.floor(upright_slot * 0.25) == group
    point_ref[0, 192:256, 0:128] = jnp.where(mine & (lane % 32 == 31), code, 0.0).astype(bf16)
    point_ref[0, 192:256, 128:256] = jnp.where(mine & (lane % 32 < 18), 1.0, 0.0).astype(bf16)
    chip = jnp.where((jnp.floor(slot * 0.25) == sub.astype(f32)) & (lane < 64), 1.0, 0.0).astype(bf16)
    point_ref[1, 192:256, 0:128] = chip
    point_ref[1, 192:256, 128:256] = chip

    order = lax.broadcasted_iota(jnp.int32, (512, 128), 0) // 2
    turns = (order * az) % 4
    along = jnp.where(turns == 0, 1.0, jnp.where(turns == 2, -1.0, 0.0))
    across = jnp.where(turns == 1, 1.0, jnp.where(turns == 3, -1.0, 0.0))
    ratio = order.astype(f32) * (1.0 / ORDERS)
    first, other = slice(0, 512), slice(512, 1024)
    low_lanes, edge_lanes = slice(0, 128), slice(128, 256)
    value = along * table_ref[first, low_lanes] + across * table_ref[other, low_lanes]
    slope = ratio * (along * table_ref[other, low_lanes] - across * table_ref[first, low_lanes])
    edge_value = along * table_ref[first, edge_lanes] + across * table_ref[other, edge_lanes]
    edge_slope = ratio * (along * table_ref[other, edge_lanes] - across * table_ref[first, edge_lanes])
    kind = ((lax.broadcasted_iota(jnp.int32, (512, 128), 1) % 32) % 9) % 3
    edge = jnp.where(kind == 2, edge_slope, edge_value)
    for i, block in enumerate((value, slope, edge)):
        high, low = split(block)
        basis_ref[0, :, 128 * i:128 * i + 128] = high
        basis_ref[1, :, 128 * i:128 * i + 128] = low


def point_weights(points):
    bf16 = jnp.bfloat16
    return pl.pallas_call(
        weight_kernel,
        out_shape=(
            jax.ShapeDtypeStruct((6, 256, 256), bf16),
            jax.ShapeDtypeStruct((2, 256, 256), bf16),
            jax.ShapeDtypeStruct((2, 512, 384), bf16),
        ),
        compiler_params=GRANT,
        name="weights",
    )(points, jnp.asarray(constant_table()))


def thrice(a, b):
    return dot(a[0], b[0]) + (dot(a[1], b[0]) + dot(a[0], b[1]))


def message_kernel(nodes_ref, weight_ref, point_ref, basis_ref, out_ref):
    f32 = jnp.float32
    coefs = jnp.concatenate([nodes_ref[q].reshape(136, 128) for q in range(4)], axis=1)
    samples = thrice(split(coefs), (basis_ref[0], basis_ref[1]))
    row = lax.broadcasted_iota(jnp.int32, (136, 128), 0)
    component = jnp.where(row < 120, row // 40, (row - 120) // 5)
    pad = jnp.zeros((120, 384), f32)
    values, slopes, edges = samples[:, :128], samples[:, 128:256], samples[:, 256:]

    def spread(block):
        parts = jnp.concatenate([jnp.where(component == s, block, 0.0) for s in range(3)], axis=1)
        return split(jnp.concatenate([parts, pad], axis=0))

    by_kind = (spread(values), None, spread(slopes))
    for d in range(3):
        field = by_kind[0] if d < 2 else by_kind[2]
        rows = thrice((weight_ref[2 * d], weight_ref[2 * d + 1]), field)
        for s in range(3):
            for c in range(4):
                out_ref[pl.ds(4 * (3 * s + d) + c, 64, stride=ROWS), :] = (
                    rows[64 * c:64 * c + 64, 128 * s:128 * s + 128])

    lane = lax.broadcasted_iota(jnp.int32, (136, 128), 1)
    edges = jnp.where(((lane % 32) % 9) // 3 == component, edges, 0.0)
    edges = split(jnp.concatenate([edges, pad[:, :128]], axis=0))
    rows = thrice((point_ref[0, 0:192], point_ref[1, 0:192]), edges)
    lane = lax.broadcasted_iota(jnp.int32, (64, 128), 1)
    kind = ((lane % 32) % 9) % 3
    extra = jnp.where(kind == 0, rows[:64], jnp.where(kind == 1, rows[64:128], rows[128:]))
    extra = (extra * point_ref[0, 192:256, 128:256].astype(f32)
             + point_ref[0, 192:256, 0:128].astype(f32))
    chip = point_ref[1, 192:256, 0:64]
    high, low = split(extra)
    out_ref[pl.ds(36, 64, stride=ROWS), :] = dot(chip, high) + dot(chip, low)


def messages(nodes, *weights):
    return pl.pallas_call(
        message_kernel,
        out_shape=jax.ShapeDtypeStruct((64 * ROWS, 128), jnp.float32),
        compiler_params=GRANT,
        name="messages",
    )(nodes, *weights)


def rims_kernel(own_ref, sib_ref, first_ref, last_ref):
    lane = lax.broadcasted_iota(jnp.int32, (32, 128), 1)
    for n, ref in enumerate((own_ref, sib_ref)):
        first = jnp.zeros((32, 128), jnp.float32)
        last = jnp.zeros((32, 128), jnp.float32)
        for g in range(9):
            first = jnp.where(lane == 9 + g, ref[g, :, 0:1], first)
            last = jnp.where(lane == g, ref[g, :, 127:128], last)
        first_ref[n] = first
        last_ref[n] = last


def rims(own, sib):
    shape = jax.ShapeDtypeStruct((2, 32, 128), jnp.float32)
    return pl.pallas_call(
        rims_kernel, out_shape=(shape, shape), compiler_params=GRANT, name="rims",
    )(own, sib)


def voxel_kernel(arrived_ref, own_ref, sib_ref, before_ref, after_ref, out_ref):
    is_low = lax.axis_index("mer_2") == 0
    f32 = jnp.float32
    tail = arrived_ref[pl.ds(36, 64, stride=ROWS), :]
    lane = lax.broadcasted_iota(jnp.int32, (64, 128), 1)
    wanted = (lane % 32 + 1).astype(f32)
    sorting = jnp.concatenate(
        [
            jnp.where((lane // 32 == c // 2) & (tail[:, 32 * c + 31:32 * c + 32] == wanted), 1.0, 0.0)
            for c in range(4)
        ],
        axis=0,
    ).astype(jnp.bfloat16)

    def sorted_sum(rows):
        high, low = split(rows)
        both = lax.dot_general(
            sorting, jnp.concatenate([high, low], axis=1), (((0,), (0,)), ((), ())),
            preferred_element_type=f32,
        )
        return both[:64, :128] + both[:64, 128:]

    totals = [jnp.zeros((32, 128), f32) for _ in range(2)]
    for g in range(9):
        summed = sorted_sum(jnp.concatenate(
            [arrived_ref[pl.ds(4 * g + c, 64, stride=ROWS), :] for c in range(4)], axis=0))
        mine, theirs = own_ref[g], sib_ref[g]
        totals[0] = totals[0] + summed[:32] * jnp.where(is_low, mine, theirs)
        totals[1] = totals[1] + summed[32:] * jnp.where(is_low, theirs, mine)
    shifted = [tail] + [pltpu.roll(tail, 128 - 32 * c, 1) for c in range(1, 4)]
    ends = sorted_sum(jnp.concatenate([jnp.where(lane < 18, x, 0.0) for x in shifted], axis=0))
    own_edge, sib_edge = before_ref[0] + after_ref[0], before_ref[1] + after_ref[1]
    side = (ends[:32] * jnp.where(is_low, own_edge, sib_edge), ends[32:] * jnp.where(is_low, sib_edge, own_edge))
    out_ref[0] = totals[0]
    out_ref[1] = totals[1]
    for core in range(2):
        product = side[core]
        small = lax.broadcasted_iota(jnp.int32, (32, 128), 1)
        west = jnp.sum(jnp.where(small < 9, product, 0.0), axis=1, keepdims=True)
        east = jnp.sum(jnp.where((small >= 9) & (small < 18), product, 0.0), axis=1, keepdims=True)
        out_ref[2 + core] = jnp.where(small == 127, west, jnp.where(small == 0, east, 0.0))


def voxels(arrived, own, sib, before, after):
    f32 = jnp.float32
    return pl.pallas_call(
        voxel_kernel,
        out_shape=jax.ShapeDtypeStruct((4, 32, 128), f32),
        compiler_params=GRANT,
        name="voxels",
    )(arrived, own, sib, before, after)


def total_kernel(mine_ref, theirs_ref, base_ref, edge_ref, full, framed):
    is_low = lax.axis_index("mer_2") == 0
    low = mine_ref[0] + theirs_ref[0]
    high = mine_ref[1] + theirs_ref[1]
    raw = jnp.where(is_low, low, high)
    ends = jnp.where(is_low, mine_ref[2] + theirs_ref[2], mine_ref[3] + theirs_ref[3])
    full[0] = low
    full[1] = high
    low_first, low_last = full[0, pl.ds(0, 8, stride=4), :], full[0, pl.ds(3, 8, stride=4), :]
    high_first, high_last = full[1, pl.ds(0, 8, stride=4), :], full[1, pl.ds(3, 8, stride=4), :]
    edge_ref[...] = jnp.where(is_low, low_first, high_last)
    framed[0:8] = jnp.zeros((8, 128), jnp.float32)
    framed[8:40] = raw
    framed[40:48] = jnp.zeros((8, 128), jnp.float32)
    lane = lax.broadcasted_iota(jnp.int32, (32, 128), 1)
    row = lax.broadcasted_iota(jnp.int32, (32, 128), 0)
    west = pltpu.roll(jnp.where(lane == 127, ends, raw), 1, 1)
    east = pltpu.roll(jnp.where(lane == 0, ends, raw), 127, 1)
    neighbours = framed[4:36] + framed[12:44] + west + east
    down = jnp.where(row % 4 == 0, 0.0, framed[7:39])
    up = jnp.where(row % 4 == 3, 0.0, framed[9:41])
    neighbours = neighbours + down + up
    base_ref[...] = raw + smooth_rate * (neighbours - 6.0 * raw)
    base_ref[pl.ds(0, 8, stride=4), :] += jnp.where(is_low, 0.0, smooth_rate * low_last)
    base_ref[pl.ds(3, 8, stride=4), :] += jnp.where(is_low, smooth_rate * high_first, 0.0)


def total(mine, theirs):
    f32 = jnp.float32
    return pl.pallas_call(
        total_kernel,
        out_shape=(jax.ShapeDtypeStruct((32, 128), f32), jax.ShapeDtypeStruct((8, 128), f32)),
        scratch_shapes=[pltpu.VMEM((2, 32, 128), f32), pltpu.VMEM((48, 128), f32)],
        compiler_params=GRANT,
        name="total",
    )(mine, theirs)


def smooth_kernel(base_ref, outer_ref, out_ref):
    is_low = lax.axis_index("mer_2") == 0
    outer = smooth_rate * outer_ref[...]
    out_ref[...] = base_ref[...]
    out_ref[pl.ds(0, 8, stride=4), :] += jnp.where(is_low, outer, 0.0)
    out_ref[pl.ds(3, 8, stride=4), :] += jnp.where(is_low, 0.0, outer)


def smooth(base, outer):
    return pl.pallas_call(
        smooth_kernel,
        out_shape=jax.ShapeDtypeStruct((32, 128), jnp.float32),
        compiler_params=GRANT,
        name="smooth",
    )(base, outer)


def on_device(
    displacement,
    velocity,
    modulus,
    hoop_strength,
    coupling,
    density,
    order_count,
    point_element,
    point_local,
    azimuth_scale,
    point_owner,
    point_cell,
    adjoint_strain,
):
    count = lax.axis_size(MER)
    az_count = lax.axis_size("az")
    swap = [(0, 1), (1, 0)]
    cross = [(c, c + 1) for c in range(1, count - 1, 2)] + [(c + 1, c) for c in range(1, count - 1, 2)]
    diagonal = [(c, c - 2) for c in range(2, count, 2)] + [(c, c + 2) for c in range(1, count - 2, 2)]
    ahead = [(i, (i + 1) % az_count) for i in range(az_count)]

    own, points = pack(
        displacement.reshape(15, 8, 128), velocity.reshape(15, 8, 128),
        modulus, hoop_strength, coupling, density, order_count,
        point_element.T, point_local.T, azimuth_scale.reshape(1, 64), point_owner.reshape(1, 64),
        point_cell.reshape(1, 64),
    )
    sib = lax.ppermute(own, "mer_2", swap)
    staged, side = stage(own)
    same = lax.ppermute(side, MER, diagonal)
    message = chip_message(staged, sib)
    outer = lax.ppermute(message, MER, cross)
    final, spread = march(message, sib, outer, same)

    weights = point_weights(points)
    nodes = lax.all_to_all(spread, "az", 0, 0, tiled=True)
    outgoing = messages(nodes, *weights)
    arrived = lax.all_to_all(outgoing.reshape(64, ROWS, 1, 128), SIDES, 0, 0, tiled=True)
    arrived = arrived.reshape(64 * ROWS, 128)

    adjoint = adjoint_strain.reshape(9, 32, 128)
    adjoint_sib = lax.ppermute(adjoint, "mer_2", swap)
    first, last = rims(adjoint, adjoint_sib)
    before = lax.ppermute(last, "az", ahead)
    after = lax.ppermute(first, "az", [(b, a) for a, b in ahead])
    part = voxels(arrived, adjoint, adjoint_sib, before, after)
    base, edge = total(part, lax.ppermute(part, "mer_2", swap))
    kernel = smooth(base, lax.ppermute(edge, MER, cross))
    return final.reshape(3, 5, 8, 128), kernel.reshape(8, 4, 128)


def solution(mesh):
    torus = Mesh(mesh.devices.reshape(8, 8, 2, mesh.shape["az"]), ("mer_0", "mer_1", "mer_2", "az"))
    return jax.shard_map(
        on_device,
        mesh=torus,
        in_specs=(
            P(None, None, MER, "az"),
            P(None, None, MER, "az"),
            P(None, MER),
            P(None, MER),
            P(None, MER),
            P(None, MER),
            P(None, MER),
            P(MER, None),
            P(MER, None),
            P(MER),
            P(MER, None),
            P(MER),
            P(None, None, MER, "az"),
        ),
        out_specs=(P(None, None, MER, "az"), P(None, MER, "az")),
        check_vma=False,
    )
```
